32 devices in a mesh: fsdp: 32 (over z, y, x, core).
Axes of the slice: x: 2, y: 2, z: 4, core: 2. Of those that a mesh axis runs over, the one named last changes fastest.
Arguments:
- inputs: bfloat16 [32, 128, 512], P('fsdp'), may hold values from -8 to 8
- front_gain: bfloat16 [512], P('fsdp'), may hold values from 0.5 to 1.5
- front_shift: bfloat16 [512], P('fsdp'), may hold values from -3 to 3
- front_expand: bfloat16 [512, 2048], P('fsdp'), may hold values from -0.25 to 0.25
- front_lift: bfloat16 [2048], P('fsdp'), may hold values from -3 to 3
- front_shrink: bfloat16 [2048, 512], P('fsdp'), may hold values from -0.125 to 0.125
- front_offset: bfloat16 [512], P('fsdp'), may hold values from -3 to 3
- attend_gain: bfloat16 [512], P('fsdp'), may hold values from 0.5 to 1.5
- attend_shift: bfloat16 [512], P('fsdp'), may hold values from -3 to 3
- query_weight: bfloat16 [512, 512], P('fsdp'), may hold values from -0.25 to 0.25
- query_bias: bfloat16 [512], P('fsdp'), may hold values from -3 to 3
- key_weight: bfloat16 [512, 512], P('fsdp'), may hold values from -0.25 to 0.25
- value_weight: bfloat16 [512, 512], P('fsdp'), may hold values from -0.25 to 0.25
- value_bias: bfloat16 [512], P('fsdp'), may hold values from -3 to 3
- place_weight: bfloat16 [512, 512], P('fsdp'), may hold values from -0.25 to 0.25
- content_bias: bfloat16 [512], P('fsdp'), may hold values from -3 to 3
- place_bias: bfloat16 [512], P('fsdp'), may hold values from -3 to 3
- output_weight: bfloat16 [512, 512], P('fsdp'), may hold values from -1 to 1
- output_bias: bfloat16 [512], P('fsdp'), may hold values from -3 to 3
- module_gain: bfloat16 [512], P('fsdp'), may hold values from 0.5 to 1.5
- module_shift: bfloat16 [512], P('fsdp'), may hold values from -3 to 3
- gating_weight: bfloat16 [512, 1024], P('fsdp'), may hold values from -0.25 to 0.25
- gating_bias: bfloat16 [1024], P('fsdp'), may hold values from -3 to 3
- depth_weight: bfloat16 [512, 31], P('fsdp'), may hold values from -1 to 1
- batch_gain: bfloat16 [512], P('fsdp'), may hold values from 0.5 to 1.5
- batch_shift: bfloat16 [512], P('fsdp'), may hold values from -3 to 3
- mixer_weight: bfloat16 [512, 512], P('fsdp'), may hold values from -0.25 to 0.25
- mixer_bias: bfloat16 [512], P('fsdp'), may hold values from -3 to 3
- rear_gain: bfloat16 [512], P('fsdp'), may hold values from 0.5 to 1.5
- rear_shift: bfloat16 [512], P('fsdp'), may hold values from -3 to 3
- rear_expand: bfloat16 [512, 2048], P('fsdp'), may hold values from -0.25 to 0.25
- rear_lift: bfloat16 [2048], P('fsdp'), may hold values from -3 to 3
- rear_shrink: bfloat16 [2048, 512], P('fsdp'), may hold values from -0.125 to 0.125
- rear_offset: bfloat16 [512], P('fsdp'), may hold values from -3 to 3
- final_gain: bfloat16 [512], P('fsdp'), may hold values from 0.5 to 1.5
- final_shift: bfloat16 [512], P('fsdp'), may hold values from -3 to 3
- cotangent: bfloat16 [32, 128, 512], P('fsdp'), may hold values from -8 to 8
Outputs:
- outputs: float32 [32, 128, 512], P('fsdp')
- input_grad: float32 [32, 128, 512], P('fsdp')
- front_gain_grad: float32 [512], P('fsdp')
- front_shift_grad: float32 [512], P('fsdp')
- front_expand_grad: float32 [512, 2048], P('fsdp')
- front_lift_grad: float32 [2048], P('fsdp')
- front_shrink_grad: float32 [2048, 512], P('fsdp')
- front_offset_grad: float32 [512], P('fsdp')
- attend_gain_grad: float32 [512], P('fsdp')
- attend_shift_grad: float32 [512], P('fsdp')
- query_weight_grad: float32 [512, 512], P('fsdp')
- query_bias_grad: float32 [512], P('fsdp')
- key_weight_grad: float32 [512, 512], P('fsdp')
- value_weight_grad: float32 [512, 512], P('fsdp')
- value_bias_grad: float32 [512], P('fsdp')
- place_weight_grad: float32 [512, 512], P('fsdp')
- content_bias_grad: float32 [512], P('fsdp')
- place_bias_grad: float32 [512], P('fsdp')
- output_weight_grad: float32 [512, 512], P('fsdp')
- output_bias_grad: float32 [512], P('fsdp')
- module_gain_grad: float32 [512], P('fsdp')
- module_shift_grad: float32 [512], P('fsdp')
- gating_weight_grad: float32 [512, 1024], P('fsdp')
- gating_bias_grad: float32 [1024], P('fsdp')
- depth_weight_grad: float32 [512, 31], P('fsdp')
- batch_gain_grad: float32 [512], P('fsdp')
- batch_shift_grad: float32 [512], P('fsdp')
- mixer_weight_grad: float32 [512, 512], P('fsdp')
- mixer_bias_grad: float32 [512], P('fsdp')
- rear_gain_grad: float32 [512], P('fsdp')
- rear_shift_grad: float32 [512], P('fsdp')
- rear_expand_grad: float32 [512, 2048], P('fsdp')
- rear_lift_grad: float32 [2048], P('fsdp')
- rear_shrink_grad: float32 [2048, 512], P('fsdp')
- rear_offset_grad: float32 [512], P('fsdp')
- final_gain_grad: float32 [512], P('fsdp')
- final_shift_grad: float32 [512], P('fsdp')
The draws below stay inside these ranges and needn't reach their ends.
All inputs are finite; a program needn't handle non-finite values.
Results may differ from the reference program's by a relative error of at most 0.025.
Values may be sent and summed in bfloat16 or wider, within the bound.
No kernel may reach another device: no remote copies, remote signals or barrier semaphores. Data moves between devices by JAX's collectives and lax.ppermute only.
A program may use at most 128 MiB of HBM per device.

```python
import math
from functools import partial
import jax
import jax.numpy as jnp
from jax import lax

D = 512
HEADS = 8
FF = 2048
KERNEL = 31
LEN = 128
SEQS = 32


def rising_field(key):
    noise_key, common_key = jax.random.split(key)
    steps = jnp.arange(SEQS).astype(jnp.float32) / max(SEQS - 1, 1)
    noise = jax.random.normal(noise_key, (SEQS, LEN, D), jnp.float32)
    level = 0.25 + 1.25 * steps
    common = jax.random.normal(common_key, (SEQS, D), jnp.float32)
    return jnp.clip(noise + level[:, None, None] * common[:, None, :], -8.0, 8.0)


def draw_inputs(key, part):
    return rising_field(jax.random.fold_in(key, 11)).astype(jnp.bfloat16)


def draw_cotangent(key, part):
    return rising_field(jax.random.fold_in(key, 23)).astype(jnp.bfloat16)


def steps_of(own_key, dims, pieces, least, high):
    level, own = 1.0, jax.random.fold_in(own_key, 6)
    for position, blocks in pieces:
        steps = jnp.exp(jax.random.uniform(jax.random.fold_in(own, position), (blocks,), jnp.float32, least / len(pieces), high / len(pieces)))
        level = level * jnp.repeat(steps, dims[position] // blocks).reshape([-1 if axis == position else 1 for axis in range(len(dims))])
    return level


def normal_values(key, dims, deviation, most, shards=(), dtype=jnp.bfloat16):
    entries = jax.random.normal(key, dims, jnp.float32) * deviation
    if len(shards) > 0:
        entries = steps_of(key, dims, shards, -0.22, 0.18) * entries
    return jnp.clip(entries, min=-most, max=most).astype(dtype)


def setup_inputs(seed: int = 0) -> dict:
    key_of = jax.random.split(jax.random.key(seed), 38)
    return {
        "inputs": draw_inputs(jax.random.fold_in(key_of[37], 71), 0),
        "front_gain": jnp.clip(1.0 + 0.1 * jax.random.normal(key_of[1], (D,), jnp.float32), 0.5, 1.5).astype(jnp.bfloat16),
        "front_shift": normal_values(key_of[2], (D,), 0.3, 3.0, ((0, 32),)),
        "front_expand": normal_values(key_of[3], (D, FF), D ** -0.5, 0.25, ((0, 32),)),
        "front_lift": normal_values(key_of[4], (FF,), 0.5, 3.0, ((0, 32),)),
        "front_shrink": normal_values(key_of[5], (FF, D), FF ** -0.5, 0.125, ((0, 32),)),
        "front_offset": normal_values(key_of[6], (D,), 0.5, 3.0, ((0, 32),)),
        "attend_gain": jnp.clip(1.0 + 0.1 * jax.random.normal(key_of[7], (D,), jnp.float32), 0.5, 1.5).astype(jnp.bfloat16),
        "attend_shift": normal_values(key_of[8], (D,), 0.3, 3.0, ((0, 32),)),
        "query_weight": normal_values(key_of[9], (D, D), D ** -0.5, 0.25, ((0, 32),)),
        "query_bias": normal_values(key_of[10], (D,), 0.5, 3.0, ((0, 32),)),
        "key_weight": normal_values(key_of[11], (D, D), D ** -0.5, 0.25, ((0, 32),)),
        "value_weight": normal_values(key_of[12], (D, D), D ** -0.5, 0.25, ((0, 32),)),
        "value_bias": normal_values(key_of[13], (D,), 0.5, 3.0, ((0, 32),)),
        "place_weight": normal_values(key_of[14], (D, D), D ** -0.5, 0.25, ((0, 32),)),
        "content_bias": normal_values(key_of[15], (D,), 0.5, 3.0, ((0, 32),)),
        "place_bias": normal_values(key_of[16], (D,), 0.5, 3.0, ((0, 32),)),
        "output_weight": normal_values(key_of[17], (D, D), (D // 16) ** -0.5, 1.0, ((0, 32),)),
        "output_bias": normal_values(key_of[18], (D,), 0.5, 3.0, ((0, 32),)),
        "module_gain": jnp.clip(1.0 + 0.1 * jax.random.normal(key_of[19], (D,), jnp.float32), 0.5, 1.5).astype(jnp.bfloat16),
        "module_shift": normal_values(key_of[20], (D,), 0.3, 3.0, ((0, 32),)),
        "gating_weight": normal_values(key_of[21], (D, 2 * D), D ** -0.5, 0.25, ((0, 32),)),
        "gating_bias": normal_values(key_of[22], (2 * D,), 0.5, 3.0, ((0, 32),)),
        "depth_weight": normal_values(key_of[23], (D, KERNEL), KERNEL ** -0.5, 1.0, ((0, 32),)),
        "batch_gain": jnp.clip(1.0 + 0.1 * jax.random.normal(key_of[24], (D,), jnp.float32), 0.5, 1.5).astype(jnp.bfloat16),
        "batch_shift": normal_values(key_of[25], (D,), 0.3, 3.0, ((0, 32),)),
        "mixer_weight": normal_values(key_of[26], (D, D), D ** -0.5, 0.25, ((0, 32),)),
        "mixer_bias": normal_values(key_of[27], (D,), 0.5, 3.0, ((0, 32),)),
        "rear_gain": jnp.clip(1.0 + 0.1 * jax.random.normal(key_of[28], (D,), jnp.float32), 0.5, 1.5).astype(jnp.bfloat16),
        "rear_shift": normal_values(key_of[29], (D,), 0.3, 3.0, ((0, 32),)),
        "rear_expand": normal_values(key_of[30], (D, FF), D ** -0.5, 0.25, ((0, 32),)),
        "rear_lift": normal_values(key_of[31], (FF,), 0.5, 3.0, ((0, 32),)),
        "rear_shrink": normal_values(key_of[32], (FF, D), FF ** -0.5, 0.125, ((0, 32),)),
        "rear_offset": normal_values(key_of[33], (D,), 0.5, 3.0, ((0, 32),)),
        "final_gain": jnp.clip(1.0 + 0.1 * jax.random.normal(key_of[34], (D,), jnp.float32), 0.5, 1.5).astype(jnp.bfloat16),
        "final_shift": normal_values(key_of[35], (D,), 0.3, 3.0, ((0, 32),)),
        "cotangent": draw_cotangent(jax.random.fold_in(key_of[37], 71), 0),
    }


EPSILON = 1e-05

def rounded(value):
    return value.astype(jnp.bfloat16)

def widened(value):
    return value.astype(jnp.float32)

def product(left, right):
    return jnp.dot(left, right, preferred_element_type=jnp.float32)

def product_left(left, right):
    return jnp.dot(left.T, right, preferred_element_type=jnp.float32)

def product_right(left, right):
    return jnp.dot(left, right.T, preferred_element_type=jnp.float32)

def contract(form, left, right):
    return jnp.einsum(form, widened(left), widened(right))

def layer_norm(rows, gain, shift):
    center = lax.optimization_barrier(jnp.mean(rows, axis=-1, keepdims=True))
    spread = rows - center
    scale = lax.rsqrt(lax.optimization_barrier(jnp.mean(spread * spread, axis=-1, keepdims=True)) + EPSILON)
    return spread * scale * gain + shift

def layer_norm_back(rows, gain, shift, grad):
    _, pullback = jax.vjp(layer_norm, rows, gain, shift)
    return pullback(grad)

def swish(value):
    return value * jax.nn.sigmoid(value)

def swish_slope(value):
    sigma = jax.nn.sigmoid(value)
    return sigma * (1.0 + value * (1.0 - sigma))

def feed_forward(rows, params):
    gain, shift, expand, lift, shrink, offset = params
    normed = rounded(layer_norm(rows, widened(gain), widened(shift)))
    hidden = product(normed, expand) + widened(lift)
    active = rounded(swish(hidden))
    result = rows + 0.5 * (product(active, shrink) + widened(offset))
    return (result, (normed, hidden, active))

def feed_forward_back(rows, params, saved, grad):
    gain, shift, expand, lift, shrink, offset = params
    normed, hidden, active = saved
    half = 0.5 * grad
    half_low = rounded(half)
    grad_shrink = product_left(active, half_low)
    grad_offset = lax.optimization_barrier(jnp.sum(half, axis=0))
    grad_hidden = product_right(half_low, shrink) * swish_slope(hidden)
    hidden_low = rounded(grad_hidden)
    grad_expand = product_left(normed, hidden_low)
    grad_lift = lax.optimization_barrier(jnp.sum(grad_hidden, axis=0))
    grad_normed = product_right(hidden_low, expand)
    grad_rows, grad_gain, grad_shift = layer_norm_back(rows, widened(gain), widened(shift), grad_normed)
    return (grad + grad_rows, (grad_gain, grad_shift, grad_expand, grad_lift, grad_shrink, grad_offset))

def place_table(length, width):
    distance = widened(length - 1 - jnp.arange(2 * length))
    rates = jnp.exp(widened(jnp.arange(width // 2)) * (-2.0 * math.log(10000.0) / width))
    angles = distance[:, None] * rates[None, :]
    return rounded(jnp.concatenate([jnp.sin(angles), jnp.cos(angles)], axis=1))

def skew(full):
    length = full.shape[-2]
    leading = full.shape[:-2]
    flat = full.reshape(leading + (2 * length * length,))
    flat = flat[..., length - 1:length - 1 + length * (2 * length - 1)]
    return flat.reshape(leading + (length, 2 * length - 1))[..., :length]

def skew_back(grad_scores):
    sequences, heads, length, _ = grad_scores.shape
    base = jnp.zeros((sequences, heads, length, 2 * length), jnp.float32)
    _, pullback = jax.vjp(skew, base)
    return pullback(grad_scores)[0]

def attend_parts(rows, params, sequences):
    gain, shift, query_w, query_b, key_w, value_w, value_b, place_w, content_b, place_b, output_w, output_b = params
    width = rows.shape[1]
    length = rows.shape[0] // sequences
    depth = width // HEADS
    normed = rounded(layer_norm(rows, widened(gain), widened(shift)))
    query = product(normed, query_w) + widened(query_b)
    keys = rounded(product(normed, key_w)).reshape(sequences, length, HEADS, depth)
    values = rounded(product(normed, value_w) + widened(value_b)).reshape(sequences, length, HEADS, depth)
    table = place_table(length, width)
    places = rounded(product(table, place_w)).reshape(2 * length, HEADS, depth)
    query_u = rounded(query + widened(content_b)).reshape(sequences, length, HEADS, depth)
    query_v = rounded(query + widened(place_b)).reshape(sequences, length, HEADS, depth)
    content = contract('slhd,smhd->shlm', query_u, keys)
    positional = skew(contract('slhd,khd->shlk', query_v, places))
    scores = (content + positional) * (1.0 / math.sqrt(depth))
    return (normed, table, keys, values, places, query_u, query_v, scores)

def attention(rows, params, sequences):
    output_w, output_b = (params[10], params[11])
    parts = attend_parts(rows, params, sequences)
    values, scores = (parts[3], parts[7])
    total = jnp.log(lax.optimization_barrier(jnp.sum(jnp.exp(scores), axis=-1)))
    mixing = rounded(jnp.exp(scores - total[..., None]))
    context = rounded(contract('shlm,smhd->slhd', mixing, values).reshape(rows.shape))
    return (rows + product(context, output_w) + widened(output_b), total)

def attention_back(rows, params, sequences, total, grad):
    gain, shift, query_w, query_b, key_w, value_w, value_b, place_w, content_b, place_b, output_w, output_b = params
    normed, table, keys, values, places, query_u, query_v, scores = attend_parts(rows, params, sequences)
    width = rows.shape[1]
    length = rows.shape[0] // sequences
    depth = width // HEADS
    mixing = jnp.exp(scores - total[..., None])
    mixing_low = rounded(mixing)
    context = rounded(contract('shlm,smhd->slhd', mixing_low, values).reshape(rows.shape))
    grad_low = rounded(grad)
    grad_output_w = product_left(context, grad_low)
    grad_output_b = lax.optimization_barrier(jnp.sum(grad, axis=0))
    grad_context = rounded(product_right(grad_low, output_w)).reshape(sequences, length, HEADS, depth)
    grad_mixing = contract('slhd,smhd->shlm', grad_context, values)
    grad_values = contract('shlm,slhd->smhd', mixing_low, grad_context)
    grad_scores = mixing * (grad_mixing - lax.optimization_barrier(jnp.sum(mixing * grad_mixing, axis=-1, keepdims=True))) * (1.0 / math.sqrt(depth))
    scores_low = rounded(grad_scores)
    grad_query_u = contract('shlm,smhd->slhd', scores_low, keys)
    grad_keys = contract('shlm,slhd->smhd', scores_low, query_u)
    full_low = rounded(skew_back(grad_scores))
    grad_query_v = contract('shlk,khd->slhd', full_low, places)
    grad_places = contract('shlk,slhd->khd', full_low, query_v).reshape(2 * length, width)
    grad_place_w = jnp.dot(widened(table).T, grad_places, precision=lax.Precision.HIGHEST)
    grad_content_b = lax.optimization_barrier(jnp.sum(grad_query_u, axis=(0, 1))).reshape(width)
    grad_place_b = lax.optimization_barrier(jnp.sum(grad_query_v, axis=(0, 1))).reshape(width)
    grad_query = (grad_query_u + grad_query_v).reshape(rows.shape)
    grad_values = grad_values.reshape(rows.shape)
    query_low = rounded(grad_query)
    keys_low = rounded(grad_keys.reshape(rows.shape))
    values_low = rounded(grad_values)
    grad_query_w = product_left(normed, query_low)
    grad_query_b = lax.optimization_barrier(jnp.sum(grad_query, axis=0))
    grad_key_w = product_left(normed, keys_low)
    grad_value_w = product_left(normed, values_low)
    grad_value_b = lax.optimization_barrier(jnp.sum(grad_values, axis=0))
    grad_normed = product_right(query_low, query_w) + product_right(keys_low, key_w) + product_right(values_low, value_w)
    grad_rows, grad_gain, grad_shift = layer_norm_back(rows, widened(gain), widened(shift), grad_normed)
    grads = (grad_gain, grad_shift, grad_query_w, grad_query_b, grad_key_w, grad_value_w, grad_value_b, grad_place_w, grad_content_b, grad_place_b, grad_output_w, grad_output_b)
    return (grad + grad_rows, grads)

def depthwise(signal, kernel):
    taps = kernel.shape[1]
    reach = taps // 2
    length = signal.shape[1]
    padded = jnp.pad(signal, ((0, 0), (reach, reach), (0, 0)))
    total = padded[:, 0:length, :] * kernel[:, 0]
    for tap in range(1, taps):
        total = total + padded[:, tap:tap + length, :] * kernel[:, tap]
    return total

def gated_depthwise(gates, kernel, sequences):
    width = kernel.shape[0]
    gated = gates[:, :width] * jax.nn.sigmoid(gates[:, width:])
    return depthwise(gated.reshape(sequences, -1, width), kernel).reshape(-1, width)

def module_head(rows, params, sequences):
    gain, shift, gating_w, gating_b, depth_w = params[:5]
    normed = rounded(layer_norm(rows, widened(gain), widened(shift)))
    gates = product(normed, gating_w) + widened(gating_b)
    return (normed, gates, gated_depthwise(gates, widened(depth_w), sequences))

def module_head_back(rows, params, sequences, grad_depth, grad):
    gain, shift, gating_w, gating_b, depth_w = params[:5]
    normed = rounded(layer_norm(rows, widened(gain), widened(shift)))
    gates = product(normed, gating_w) + widened(gating_b)
    _, pullback = jax.vjp(partial(gated_depthwise, sequences=sequences), gates, widened(depth_w))
    grad_gates, grad_kernel = pullback(grad_depth)
    gates_low = rounded(grad_gates)
    grad_gating_w = product_left(normed, gates_low)
    grad_gating_b = lax.optimization_barrier(jnp.sum(grad_gates, axis=0))
    grad_normed = product_right(gates_low, gating_w)
    grad_rows, grad_gain, grad_shift = layer_norm_back(rows, widened(gain), widened(shift), grad_normed)
    return (grad + grad_rows, (grad_gain, grad_shift, grad_gating_w, grad_gating_b, grad_kernel))

def module_tail(rows, depth_out, params, center, inverse_root):
    batch_gain, batch_shift, mixer_w, mixer_b = params[5:]
    normal = (depth_out - center) * inverse_root
    batch_out = normal * widened(batch_gain) + widened(batch_shift)
    activated = rounded(swish(batch_out))
    return (rows + product(activated, mixer_w) + widened(mixer_b), (normal, batch_out, activated))

def module_tail_back(params, saved, grad):
    batch_gain, batch_shift, mixer_w, mixer_b = params[5:]
    normal, batch_out, activated = saved
    grad_low = rounded(grad)
    grad_mixer_w = product_left(activated, grad_low)
    grad_mixer_b = lax.optimization_barrier(jnp.sum(grad, axis=0))
    grad_batch = product_right(grad_low, mixer_w) * swish_slope(batch_out)
    grad_batch_gain = lax.optimization_barrier(jnp.sum(grad_batch * normal, axis=0))
    grad_batch_shift = lax.optimization_barrier(jnp.sum(grad_batch, axis=0))
    grad_normal = grad_batch * widened(batch_gain)
    return (grad_normal, (grad_batch_gain, grad_batch_shift, grad_mixer_w, grad_mixer_b))

def reference(inputs, front_gain, front_shift, front_expand, front_lift, front_shrink, front_offset, attend_gain, attend_shift, query_weight, query_bias, key_weight, value_weight, value_bias, place_weight, content_bias, place_bias, output_weight, output_bias, module_gain, module_shift, gating_weight, gating_bias, depth_weight, batch_gain, batch_shift, mixer_weight, mixer_bias, rear_gain, rear_shift, rear_expand, rear_lift, rear_shrink, rear_offset, final_gain, final_shift, cotangent):
    front = (front_gain, front_shift, front_expand, front_lift, front_shrink, front_offset)
    attend = (attend_gain, attend_shift, query_weight, query_bias, key_weight, value_weight, value_bias, place_weight, content_bias, place_bias, output_weight, output_bias)
    module = (module_gain, module_shift, gating_weight, gating_bias, depth_weight, batch_gain, batch_shift, mixer_weight, mixer_bias)
    rear = (rear_gain, rear_shift, rear_expand, rear_lift, rear_shrink, rear_offset)
    group = math.gcd(SEQS, max(1, 4096 // LEN))
    blocks = SEQS // group
    count = SEQS * LEN
    rows_all = widened(inputs).reshape(blocks, group * LEN, D)
    cot_all = widened(cotangent).reshape(blocks, group * LEN, D)

    def section_one(rows):
        first = feed_forward(rows, front)[0]
        second, total = attention(first, attend, group)
        depth_out = module_head(second, module, group)[2]
        return (first, second, total, depth_out)
    first_all, second_all, total_all, depth_all = lax.map(section_one, rows_all)
    center = lax.optimization_barrier(jnp.sum(depth_all, axis=(0, 1))) / count
    inverse_root = lax.rsqrt(lax.optimization_barrier(jnp.sum(depth_all * depth_all, axis=(0, 1))) / count - center * center + EPSILON)

    def section_two(block):
        second, depth_out, cot = block
        third, tail_saved = module_tail(second, depth_out, module, center, inverse_root)
        fourth, rear_saved = feed_forward(third, rear)
        gain, shift = (widened(final_gain), widened(final_shift))
        outputs = layer_norm(fourth, gain, shift)
        grad_fourth, grad_final_gain, grad_final_shift = layer_norm_back(fourth, gain, shift, cot)
        grad_third, rear_grads = feed_forward_back(third, rear, rear_saved, grad_fourth)
        grad_normal, tail_grads = module_tail_back(module, tail_saved, grad_third)
        return (outputs, grad_third, grad_normal, rear_grads + (grad_final_gain, grad_final_shift), tail_grads)
    outputs_all, third_grad_all, normal_grad_all, rear_stack, tail_stack = lax.map(section_two, (second_all, depth_all, cot_all))
    normal_all = (depth_all - center) * inverse_root
    normal_sum = lax.optimization_barrier(jnp.sum(normal_grad_all, axis=(0, 1)))
    cross_sum = lax.optimization_barrier(jnp.sum(normal_grad_all * normal_all, axis=(0, 1)))

    def section_three(block):
        rows, first, second, total, depth_out, grad_third, grad_normal = block
        normal = (depth_out - center) * inverse_root
        grad_depth = inverse_root * (grad_normal - normal_sum / count - normal * (cross_sum / count))
        grad_second, head_grads = module_head_back(second, module, group, grad_depth, grad_third)
        grad_first, attend_grads = attention_back(first, attend, group, total, grad_second)
        grad_input, front_grads = feed_forward_back(rows, front, feed_forward(rows, front)[1], grad_first)
        return (grad_input, front_grads, attend_grads, head_grads)
    input_all, front_stack, attend_stack, head_stack = lax.map(section_three, (rows_all, first_all, second_all, total_all, depth_all, third_grad_all, normal_grad_all))

    def summed(stack):
        return tuple((lax.optimization_barrier(jnp.sum(item, axis=0)) for item in stack))
    grads = summed(front_stack) + summed(attend_stack) + summed(head_stack) + summed(tail_stack) + summed(rear_stack)
    return (outputs_all.reshape(SEQS, LEN, D), input_all.reshape(SEQS, LEN, D)) + grads
```

```python
from functools import partial
import math

import jax
import jax.numpy as jnp
from jax import lax
from jax.experimental import pallas as pl
from jax.experimental.pallas import tpu as pltpu
from jax.sharding import PartitionSpec as P

HEADS = 8


EPSILON = 1e-05


def rounded(value):
    return value.astype(jnp.bfloat16)


def widened(value):
    return value.astype(jnp.float32)


def product(left, right):
    return jnp.dot(left, right, preferred_element_type=jnp.float32)


def product_left(left, right):
    return jnp.dot(left.T, right, preferred_element_type=jnp.float32)


def product_right(left, right):
    return jnp.dot(left, right.T, preferred_element_type=jnp.float32)


def contract(form, left, right):
    return jnp.einsum(form, left, right, preferred_element_type=jnp.float32)


def layer_norm(rows, gain, shift):
    center = jnp.mean(rows, axis=-1, keepdims=True)
    spread = rows - center
    scale = lax.rsqrt(jnp.mean(spread * spread, axis=-1, keepdims=True) + EPSILON)
    return spread * scale * gain + shift


def layer_norm_back(rows, gain, shift, grad):
    _, pullback = jax.vjp(layer_norm, rows, gain, shift)
    return pullback(grad)


def swish(value):
    return value * jax.nn.sigmoid(value)


def swish_slope(value):
    sigma = jax.nn.sigmoid(value)
    return sigma * (1.0 + value * (1.0 - sigma))


def feed_forward(rows, params):
    gain, shift, expand, lift, shrink, offset = params
    normed = rounded(layer_norm(rows, widened(gain), widened(shift)))
    hidden = product(normed, expand) + widened(lift)
    active = rounded(swish(hidden))
    result = rows + 0.5 * (product(active, shrink) + widened(offset))
    return (result, (normed, hidden, active))


def feed_forward_back(rows, params, saved, grad):
    gain, shift, expand, lift, shrink, offset = params
    normed, hidden, active = saved
    half = 0.5 * grad
    half_low = rounded(half)
    grad_shrink = product_left(active, half_low)
    grad_offset = jnp.sum(half, axis=0)
    grad_hidden = product_right(half_low, shrink) * swish_slope(hidden)
    hidden_low = rounded(grad_hidden)
    grad_expand = product_left(normed, hidden_low)
    grad_lift = jnp.sum(grad_hidden, axis=0)
    grad_normed = product_right(hidden_low, expand)
    grad_rows, grad_gain, grad_shift = layer_norm_back(
        rows, widened(gain), widened(shift), grad_normed
    )
    return (
        grad + grad_rows,
        (grad_gain, grad_shift, grad_expand, grad_lift, grad_shrink, grad_offset),
    )


def place_table(length, width):
    distance = widened(length - 1 - jnp.arange(2 * length))
    rates = jnp.exp(widened(jnp.arange(width // 2)) * (-2.0 * math.log(10000.0) / width))
    angles = distance[:, None] * rates[None, :]
    return rounded(jnp.concatenate([jnp.sin(angles), jnp.cos(angles)], axis=1))


def skew(full):
    length = full.shape[-2]
    leading = full.shape[:-2]
    flat = full.reshape(leading + (2 * length * length,))
    flat = flat[..., length - 1 : length - 1 + length * (2 * length - 1)]
    return flat.reshape(leading + (length, 2 * length - 1))[..., :length]


def skew_back(grad_scores):
    sequences, heads, length, _ = grad_scores.shape
    base = jnp.zeros((sequences, heads, length, 2 * length), jnp.float32)
    _, pullback = jax.vjp(skew, base)
    return pullback(grad_scores)[0]


def attend_parts(rows, params, sequences):
    (
        gain,
        shift,
        query_w,
        query_b,
        key_w,
        value_w,
        value_b,
        place_w,
        content_b,
        place_b,
        output_w,
        output_b,
    ) = params
    width = rows.shape[1]
    length = rows.shape[0] // sequences
    depth = width // HEADS
    normed = rounded(layer_norm(rows, widened(gain), widened(shift)))
    query = product(normed, query_w) + widened(query_b)
    keys = rounded(product(normed, key_w)).reshape(sequences, length, HEADS, depth)
    values = rounded(product(normed, value_w) + widened(value_b)).reshape(
        sequences, length, HEADS, depth
    )
    table = place_table(length, width)
    places = rounded(product(table, place_w)).reshape(2 * length, HEADS, depth)
    query_u = rounded(query + widened(content_b)).reshape(sequences, length, HEADS, depth)
    query_v = rounded(query + widened(place_b)).reshape(sequences, length, HEADS, depth)
    content = contract("slhd,smhd->shlm", query_u, keys)
    positional = skew(contract("slhd,khd->shlk", query_v, places))
    scores = (content + positional) * (1.0 / math.sqrt(depth))
    return (normed, table, keys, values, places, query_u, query_v, scores)


def attention(rows, params, sequences):
    output_w, output_b = (params[10], params[11])
    parts = attend_parts(rows, params, sequences)
    values, scores = (parts[3], parts[7])
    total = jnp.log(jnp.sum(jnp.exp(scores), axis=-1))
    mixing = rounded(jnp.exp(scores - total[..., None]))
    context = rounded(contract("shlm,smhd->slhd", mixing, values).reshape(rows.shape))
    return (rows + product(context, output_w) + widened(output_b), total)


def attention_back(rows, params, sequences, total, grad):
    (
        gain,
        shift,
        query_w,
        query_b,
        key_w,
        value_w,
        value_b,
        place_w,
        content_b,
        place_b,
        output_w,
        output_b,
    ) = params
    normed, table, keys, values, places, query_u, query_v, scores = attend_parts(
        rows, params, sequences
    )
    width = rows.shape[1]
    length = rows.shape[0] // sequences
    depth = width // HEADS
    mixing = jnp.exp(scores - total[..., None])
    mixing_low = rounded(mixing)
    context = rounded(contract("shlm,smhd->slhd", mixing_low, values).reshape(rows.shape))
    grad_low = rounded(grad)
    grad_output_w = product_left(context, grad_low)
    grad_output_b = jnp.sum(grad, axis=0)
    grad_context = rounded(product_right(grad_low, output_w)).reshape(
        sequences, length, HEADS, depth
    )
    grad_mixing = contract("slhd,smhd->shlm", grad_context, values)
    grad_values = contract("shlm,slhd->smhd", mixing_low, grad_context)
    grad_scores = (
        mixing
        * (grad_mixing - jnp.sum(mixing * grad_mixing, axis=-1, keepdims=True))
        * (1.0 / math.sqrt(depth))
    )
    scores_low = rounded(grad_scores)
    grad_query_u = contract("shlm,smhd->slhd", scores_low, keys)
    grad_keys = contract("shlm,slhd->smhd", scores_low, query_u)
    full_low = rounded(skew_back(grad_scores))
    grad_query_v = contract("shlk,khd->slhd", full_low, places)
    grad_places = contract("shlk,slhd->khd", full_low, query_v).reshape(2 * length, width)
    grad_place_w = jnp.dot(widened(table).T, grad_places, precision=lax.Precision.HIGHEST)
    grad_content_b = jnp.sum(grad_query_u, axis=(0, 1)).reshape(width)
    grad_place_b = jnp.sum(grad_query_v, axis=(0, 1)).reshape(width)
    grad_query = (grad_query_u + grad_query_v).reshape(rows.shape)
    grad_values = grad_values.reshape(rows.shape)
    query_low = rounded(grad_query)
    keys_low = rounded(grad_keys.reshape(rows.shape))
    values_low = rounded(grad_values)
    grad_query_w = product_left(normed, query_low)
    grad_query_b = jnp.sum(grad_query, axis=0)
    grad_key_w = product_left(normed, keys_low)
    grad_value_w = product_left(normed, values_low)
    grad_value_b = jnp.sum(grad_values, axis=0)
    grad_normed = (
        product_right(query_low, query_w)
        + product_right(keys_low, key_w)
        + product_right(values_low, value_w)
    )
    grad_rows, grad_gain, grad_shift = layer_norm_back(
        rows, widened(gain), widened(shift), grad_normed
    )
    grads = (
        grad_gain,
        grad_shift,
        grad_query_w,
        grad_query_b,
        grad_key_w,
        grad_value_w,
        grad_value_b,
        grad_place_w,
        grad_content_b,
        grad_place_b,
        grad_output_w,
        grad_output_b,
    )
    return (grad + grad_rows, grads)


def depthwise(signal, kernel):
    taps = kernel.shape[1]
    reach = taps // 2
    length = signal.shape[1]
    padded = jnp.pad(signal, ((0, 0), (reach, reach), (0, 0)))
    total = padded[:, 0:length, :] * kernel[:, 0]
    for tap in range(1, taps):
        total = total + padded[:, tap : tap + length, :] * kernel[:, tap]
    return total


def gated_depthwise(gates, kernel, sequences):
    width = kernel.shape[0]
    gated = gates[:, :width] * jax.nn.sigmoid(gates[:, width:])
    return depthwise(gated.reshape(sequences, -1, width), kernel).reshape(-1, width)


def module_head(rows, params, sequences):
    gain, shift, gating_w, gating_b, depth_w = params[:5]
    normed = rounded(layer_norm(rows, widened(gain), widened(shift)))
    gates = product(normed, gating_w) + widened(gating_b)
    return (normed, gates, gated_depthwise(gates, widened(depth_w), sequences))


def module_head_back(rows, params, sequences, grad_depth, grad):
    gain, shift, gating_w, gating_b, depth_w = params[:5]
    normed = rounded(layer_norm(rows, widened(gain), widened(shift)))
    gates = product(normed, gating_w) + widened(gating_b)
    _, pullback = jax.vjp(partial(gated_depthwise, sequences=sequences), gates, widened(depth_w))
    grad_gates, grad_kernel = pullback(grad_depth)
    gates_low = rounded(grad_gates)
    grad_gating_w = product_left(normed, gates_low)
    grad_gating_b = jnp.sum(grad_gates, axis=0)
    grad_normed = product_right(gates_low, gating_w)
    grad_rows, grad_gain, grad_shift = layer_norm_back(
        rows, widened(gain), widened(shift), grad_normed
    )
    return (grad + grad_rows, (grad_gain, grad_shift, grad_gating_w, grad_gating_b, grad_kernel))


def module_tail(rows, depth_out, params, center, inverse_root):
    batch_gain, batch_shift, mixer_w, mixer_b = params[5:]
    normal = (depth_out - center) * inverse_root
    batch_out = normal * widened(batch_gain) + widened(batch_shift)
    activated = rounded(swish(batch_out))
    return (rows + product(activated, mixer_w) + widened(mixer_b), (normal, batch_out, activated))


def module_tail_back(params, saved, grad):
    batch_gain, batch_shift, mixer_w, mixer_b = params[5:]
    normal, batch_out, activated = saved
    grad_low = rounded(grad)
    grad_mixer_w = product_left(activated, grad_low)
    grad_mixer_b = jnp.sum(grad, axis=0)
    grad_batch = product_right(grad_low, mixer_w) * swish_slope(batch_out)
    grad_batch_gain = jnp.sum(grad_batch * normal, axis=0)
    grad_batch_shift = jnp.sum(grad_batch, axis=0)
    grad_normal = grad_batch * widened(batch_gain)
    return (grad_normal, (grad_batch_gain, grad_batch_shift, grad_mixer_w, grad_mixer_b))


def pack_early(front, attend):
    vectors = jnp.stack(
        [
            front[0],
            front[1],
            front[5],
            attend[0],
            attend[1],
            attend[3],
            attend[6],
            attend[8],
            attend[9],
            attend[11],
        ],
        axis=0,
    )
    joined = jnp.concatenate([attend[2], attend[4], attend[5], attend[7], attend[10]], axis=1)
    return (vectors, front[3], front[2], front[4], joined)


def unpack_early(packed):
    vectors, lift, expand, shrink, joined = packed
    span = joined.shape[1] // 5
    front = (vectors[0], vectors[1], expand, lift, shrink, vectors[2])
    attend = (
        vectors[3],
        vectors[4],
        joined[:, 0:span],
        vectors[5],
        joined[:, span : 2 * span],
        joined[:, 2 * span : 3 * span],
        vectors[6],
        joined[:, 3 * span : 4 * span],
        vectors[7],
        vectors[8],
        joined[:, 4 * span : 5 * span],
        vectors[9],
    )
    return (front, attend)


def pack_module(module):
    vectors = jnp.stack([module[0], module[1], module[5], module[6], module[8]], axis=0)
    joined = jnp.concatenate([module[2], module[7]], axis=1)
    return (vectors, module[3], joined, module[4])


def unpack_module(packed):
    vectors, gating_b, joined, kernel = packed
    span = joined.shape[1] // 3
    return (
        vectors[0],
        vectors[1],
        joined[:, 0 : 2 * span],
        gating_b,
        kernel,
        vectors[2],
        vectors[3],
        joined[:, 2 * span : 3 * span],
        vectors[4],
    )


def pack_rear(rear, closing):
    vectors = jnp.stack([rear[0], rear[1], rear[5], closing[0], closing[1]], axis=0)
    return (vectors, rear[3], rear[2], rear[4])


def unpack_rear(packed):
    vectors, lift, expand, shrink = packed
    return ((vectors[0], vectors[1], expand, lift, shrink, vectors[2]), (vectors[3], vectors[4]))


def local_plain(
    inputs,
    front_gain,
    front_shift,
    front_expand,
    front_lift,
    front_shrink,
    front_offset,
    attend_gain,
    attend_shift,
    query_weight,
    query_bias,
    key_weight,
    value_weight,
    value_bias,
    place_weight,
    content_bias,
    place_bias,
    output_weight,
    output_bias,
    module_gain,
    module_shift,
    gating_weight,
    gating_bias,
    depth_weight,
    batch_gain,
    batch_shift,
    mixer_weight,
    mixer_bias,
    rear_gain,
    rear_shift,
    rear_expand,
    rear_lift,
    rear_shrink,
    rear_offset,
    final_gain,
    final_shift,
    cotangent,
):
    sequences, length, width = inputs.shape
    count = lax.axis_size("fsdp") * sequences * length
    rows = widened(inputs).reshape(sequences * length, width)
    front_own = (front_gain, front_shift, front_expand, front_lift, front_shrink, front_offset)
    attend_own = (
        attend_gain,
        attend_shift,
        query_weight,
        query_bias,
        key_weight,
        value_weight,
        value_bias,
        place_weight,
        content_bias,
        place_bias,
        output_weight,
        output_bias,
    )
    module_own = (
        module_gain,
        module_shift,
        gating_weight,
        gating_bias,
        depth_weight,
        batch_gain,
        batch_shift,
        mixer_weight,
        mixer_bias,
    )
    rear_own = (rear_gain, rear_shift, rear_expand, rear_lift, rear_shrink, rear_offset)
    early_own = pack_early(front_own, attend_own)
    early = (
        lax.all_gather(early_own[0], "fsdp", axis=1, tiled=True),
        lax.all_gather(early_own[1], "fsdp", axis=0, tiled=True),
        lax.all_gather(early_own[2], "fsdp", axis=0, tiled=True),
        lax.all_gather(early_own[3], "fsdp", axis=0, tiled=True),
        lax.all_gather(early_own[4], "fsdp", axis=0, tiled=True),
    )
    front, attend = unpack_early(early)
    first = feed_forward(rows, front)[0]
    module_pack = pack_module(module_own)
    rear_pack = pack_rear(rear_own, (final_gain, final_shift))
    late = (
        lax.all_gather(module_pack[0], "fsdp", axis=1, tiled=True),
        lax.all_gather(module_pack[1], "fsdp", axis=0, tiled=True),
        lax.all_gather(module_pack[2], "fsdp", axis=0, tiled=True),
        lax.all_gather(module_pack[3], "fsdp", axis=0, tiled=True),
        lax.all_gather(rear_pack[0], "fsdp", axis=1, tiled=True),
        lax.all_gather(rear_pack[1], "fsdp", axis=0, tiled=True),
        lax.all_gather(rear_pack[2], "fsdp", axis=0, tiled=True),
        lax.all_gather(rear_pack[3], "fsdp", axis=0, tiled=True),
    )
    second, total = attention(first, attend, sequences)
    module = unpack_module(late[0:4])
    rear, closing = unpack_rear(late[4:8])
    depth_out = module_head(second, module, sequences)[2]
    first_sum, square_sum = lax.psum(
        (jnp.sum(depth_out, axis=0), jnp.sum(depth_out * depth_out, axis=0)), "fsdp"
    )
    center = first_sum / count
    inverse_root = lax.rsqrt(square_sum / count - center * center + EPSILON)
    third, tail_saved = module_tail(second, depth_out, module, center, inverse_root)
    fourth, rear_saved = feed_forward(third, rear)
    closing_gain, closing_shift = (widened(closing[0]), widened(closing[1]))
    outputs = layer_norm(fourth, closing_gain, closing_shift)
    grad_fourth, grad_final_gain, grad_final_shift = layer_norm_back(
        fourth, closing_gain, closing_shift, widened(cotangent).reshape(sequences * length, width)
    )
    grad_third, rear_grads = feed_forward_back(third, rear, rear_saved, grad_fourth)
    again = (
        lax.all_gather(early_own[0], "fsdp", axis=1, tiled=True),
        lax.all_gather(early_own[1], "fsdp", axis=0, tiled=True),
        lax.all_gather(early_own[2], "fsdp", axis=0, tiled=True),
        lax.all_gather(early_own[3], "fsdp", axis=0, tiled=True),
        lax.all_gather(early_own[4], "fsdp", axis=0, tiled=True),
        lax.all_gather(module_pack[0], "fsdp", axis=1, tiled=True),
        lax.all_gather(module_pack[1], "fsdp", axis=0, tiled=True),
        lax.all_gather(module_pack[2], "fsdp", axis=0, tiled=True),
        lax.all_gather(module_pack[3], "fsdp", axis=0, tiled=True),
    )
    front_again, attend_again = unpack_early(again[0:5])
    module_again = unpack_module(again[5:9])
    grad_normal, tail_grads = module_tail_back(module_again, tail_saved, grad_third)
    normal = tail_saved[0]
    normal_sum, cross_sum = lax.psum(
        (jnp.sum(grad_normal, axis=0), jnp.sum(grad_normal * normal, axis=0)), "fsdp"
    )
    grad_depth = inverse_root * (grad_normal - normal_sum / count - normal * (cross_sum / count))
    grad_second, head_grads = module_head_back(
        second, module_again, sequences, grad_depth, grad_third
    )
    module_all = head_grads + tail_grads
    late_grad_pack = pack_module(module_all) + pack_rear(
        rear_grads, (grad_final_gain, grad_final_shift)
    )
    late_done = (
        lax.psum_scatter(late_grad_pack[0], "fsdp", scatter_dimension=1, tiled=True),
        lax.psum_scatter(late_grad_pack[1], "fsdp", scatter_dimension=0, tiled=True),
        lax.psum_scatter(late_grad_pack[2], "fsdp", scatter_dimension=0, tiled=True),
        lax.psum_scatter(late_grad_pack[3], "fsdp", scatter_dimension=0, tiled=True),
        lax.psum_scatter(late_grad_pack[4], "fsdp", scatter_dimension=1, tiled=True),
        lax.psum_scatter(late_grad_pack[5], "fsdp", scatter_dimension=0, tiled=True),
        lax.psum_scatter(late_grad_pack[6], "fsdp", scatter_dimension=0, tiled=True),
        lax.psum_scatter(late_grad_pack[7], "fsdp", scatter_dimension=0, tiled=True),
    )
    grad_first, attend_all = attention_back(first, attend_again, sequences, total, grad_second)
    grad_input, front_all = feed_forward_back(
        rows, front_again, feed_forward(rows, front_again)[1], grad_first
    )
    early_grad_pack = pack_early(front_all, attend_all)
    early_done = (
        lax.psum_scatter(early_grad_pack[0], "fsdp", scatter_dimension=1, tiled=True),
        lax.psum_scatter(early_grad_pack[1], "fsdp", scatter_dimension=0, tiled=True),
        lax.psum_scatter(early_grad_pack[2], "fsdp", scatter_dimension=0, tiled=True),
        lax.psum_scatter(early_grad_pack[3], "fsdp", scatter_dimension=0, tiled=True),
        lax.psum_scatter(early_grad_pack[4], "fsdp", scatter_dimension=0, tiled=True),
    )
    front_out, attend_out = unpack_early(early_done)
    module_out = unpack_module(late_done[0:4])
    rear_out, closing_out = unpack_rear(late_done[4:8])
    return (
        (outputs.reshape(sequences, length, width), grad_input.reshape(sequences, length, width))
        + tuple(front_out)
        + tuple(attend_out)
        + tuple(module_out)
        + tuple(rear_out)
        + tuple(closing_out)
    )


AXIS = "fsdp"
TILE_ROWS = 16


def swap(value, bit, devices):
    return lax.ppermute(value, AXIS, [(i, i ^ bit) for i in range(devices)])


def stage_orders(devices):
    order = []
    bit = devices // 2
    while bit >= 1:
        order.append(bit)
        bit //= 2
    other = list(order)
    other[-3], other[-2] = other[-2], other[-3]
    return order, other


def relative(position, order):
    total = 0
    for place, bit in enumerate(order[:-1]):
        if (position >> place) & 1:
            total ^= bit
    return total


def gather_bundle(block_a, block_b, devices):
    order_a, order_b = stage_orders(devices)
    heads = len(order_a) - 3
    split = block_a.shape[0]
    both = jnp.concatenate([block_a, block_b], axis=0)[None]
    for bit in order_a[:heads]:
        both = jnp.concatenate([both, swap(both, bit, devices)], axis=0)
    part_a, part_b = both[:, :split], both[:, split:]
    for bit_a, bit_b in zip(order_a[heads:-1], order_b[heads:-1]):
        next_a, next_b = swap(part_a, bit_a, devices), swap(part_b, bit_b, devices)
        part_a = jnp.concatenate([part_a, next_a], axis=0)
        part_b = jnp.concatenate([part_b, next_b], axis=0)
    return (part_a, swap(part_a, 1, devices), part_b, swap(part_b, 1, devices))


def reduce_bundle(halves, devices):
    keep_a, send_a, keep_b, send_b = halves
    order_a, order_b = stage_orders(devices)
    heads = len(order_a) - 3
    got_a, got_b = swap(send_a, 1, devices), swap(send_b, 1, devices)

    def step(keep, got, bit):
        half = keep.shape[0] // 2
        send = rounded(widened(keep[half:]) + widened(got[half:]))
        arrived = swap(send, bit, devices)
        return rounded(widened(keep[:half]) + widened(got[:half])), arrived

    for bit_a, bit_b in zip(order_a[heads:-1][::-1], order_b[heads:-1][::-1]):
        keep_a, got_a = step(keep_a, got_a, bit_a)
        keep_b, got_b = step(keep_b, got_b, bit_b)
    keep = jnp.concatenate([keep_a, keep_b], axis=1)
    got = jnp.concatenate([got_a, got_b], axis=1)
    for bit in order_a[:heads][::-1]:
        keep, got = step(keep, got, bit)
    return (widened(keep) + widened(got))[0]


def sum_all(value, devices):
    bit = 1
    while bit < devices:
        value = value + swap(value, bit, devices)
        bit *= 2
    return value


def block_of(weight, width):
    blocks = weight.shape[1] // width
    return [weight[:, k * width : (k + 1) * width] for k in range(blocks)]


def plan_of(shapes, width):
    plan, offset = [], 0
    for rows, columns in shapes:
        blocks = columns // width
        plan.append((rows, blocks, offset))
        offset += rows * blocks
    return plan


def spread_kernel(devices, width, plans, vector, me_ref, *refs):
    halves, outs = refs[:4], refs[4:]
    orders = stage_orders(devices)
    me = me_ref[0]
    for colour in range(2):
        base = colour * len(plans[0])
        for core in range(2):
            source = halves[2 * colour + core]
            for position in range(devices // 2):
                owner = me ^ (relative(position, orders[colour]) ^ core)
                for item, (rows, blocks, offset) in enumerate(plans[colour]):
                    start = pl.multiple_of(owner * rows, rows)
                    for k in range(blocks):
                        outs[base + item][pl.ds(start, rows), k * width : (k + 1) * width] = source[
                            position, offset + k * rows : offset + (k + 1) * rows, :
                        ]
                if vector is not None and colour == 0:
                    start = pl.multiple_of(owner * TILE_ROWS, TILE_ROWS)
                    refs[-1][pl.ds(start, TILE_ROWS), :] = source[position, vector : vector + TILE_ROWS, :]
    if vector is not None:
        table, lifts, bias, held = refs[-4:]
        own = width // devices
        groups = width // 128
        for owner in range(devices):
            tile = widened(held[owner * TILE_ROWS : (owner + 1) * TILE_ROWS, :])
            for k in range(groups):
                table[k * TILE_ROWS : (k + 1) * TILE_ROWS, owner * own : (owner + 1) * own] = tile[
                    :, k * 128 : k * 128 + own
                ]
            lifts[:, owner * 4 * own : (owner + 1) * 4 * own] = tile[4:6, 128 : 128 + 4 * own]
            bias[:, owner * 2 * own : (owner + 1) * 2 * own] = tile[6:7, 128 : 128 + 2 * own]


def spread(me, halves, shapes_a, shapes_b, width, devices, vector=None):
    plans = (plan_of(shapes_a, width), plan_of(shapes_b, width))
    out_shape = [
        jax.ShapeDtypeStruct((devices * rows, columns), jnp.bfloat16) for rows, columns in shapes_a + shapes_b
    ]
    scratch = []
    if vector is not None:
        out_shape += [
            jax.ShapeDtypeStruct((width // 128 * TILE_ROWS, width), jnp.float32),
            jax.ShapeDtypeStruct((2, 4 * width), jnp.float32),
            jax.ShapeDtypeStruct((1, 2 * width), jnp.float32),
        ]
        scratch = [pltpu.VMEM((devices * TILE_ROWS, width), jnp.bfloat16)]
    return pl.pallas_call(
        partial(spread_kernel, devices, width, plans, vector),
        out_shape=out_shape,
        in_specs=[pl.BlockSpec(memory_space=pltpu.SMEM)] + [pl.BlockSpec(memory_space=pltpu.VMEM)] * 4,
        out_specs=[pl.BlockSpec(memory_space=pltpu.VMEM)] * len(out_shape),
        scratch_shapes=scratch,
        name="spread",
    )(me, *halves)


def collect_kernel(devices, width, plans, me_ref, *refs):
    count = len(plans[0]) + len(plans[1])
    sources, halves = refs[:count], refs[count:]
    orders = stage_orders(devices)
    me = me_ref[0]
    for colour in range(2):
        base = colour * len(plans[0])
        for core in range(2):
            target = halves[2 * colour + core]
            for position in range(devices // 2):
                owner = me ^ (relative(position, orders[colour]) ^ core)
                for item, (rows, blocks, offset) in enumerate(plans[colour]):
                    start = pl.multiple_of(owner * rows, rows)
                    for k in range(blocks):
                        target[position, offset + k * rows : offset + (k + 1) * rows, :] = rounded(
                            sources[base + item][pl.ds(start, rows), k * width : (k + 1) * width]
                        )


def collect(me, grads_a, grads_b, width, devices):
    shapes = [[(g.shape[0] // devices, g.shape[1]) for g in grads] for grads in (grads_a, grads_b)]
    plans = tuple(plan_of(s, width) for s in shapes)
    heights = [sum(rows * blocks for rows, blocks, _ in plan) for plan in plans]
    out_shape = [
        jax.ShapeDtypeStruct((devices // 2, heights[colour], width), jnp.bfloat16) for colour in (0, 0, 1, 1)
    ]
    operands = list(grads_a) + list(grads_b)
    return pl.pallas_call(
        partial(collect_kernel, devices, width, plans),
        out_shape=out_shape,
        in_specs=[pl.BlockSpec(memory_space=pltpu.SMEM)] + [pl.BlockSpec(memory_space=pltpu.VMEM)] * len(operands),
        out_specs=[pl.BlockSpec(memory_space=pltpu.VMEM)] * 4,
        name="collect",
    )(me, *operands)


def shard_of(rows, shapes, width):
    shards, offset = [], 0
    for height, columns in shapes:
        blocks = columns // width
        pieces = [rows[offset + k * height : offset + (k + 1) * height] for k in range(blocks)]
        shards.append(pieces[0] if blocks == 1 else jnp.concatenate(pieces, axis=1))
        offset += height * blocks
    return shards


def own_of(rows, me, own):
    return lax.dynamic_slice(rows, (0, me * own), (rows.shape[0], own))


def attention_parts(rows, params, sequences):
    output_w, output_b = params[10], params[11]
    parts = attend_parts(rows, params, sequences)
    values, scores = parts[3], parts[7]
    total = jnp.log(jnp.sum(jnp.exp(scores), axis=-1))
    mixing = jnp.exp(scores - total[..., None])
    mixing_low = rounded(mixing)
    context = rounded(contract("shlm,smhd->slhd", mixing_low, values).reshape(rows.shape))
    result = rows + product(context, output_w) + widened(output_b)
    return result, parts[:7] + (mixing, mixing_low, context)


def taps_depthwise(gates, taps, sequences):
    width = taps.shape[1]
    gated = (gates[:, :width] * jax.nn.sigmoid(gates[:, width:])).reshape(sequences, -1, width)
    count, length = taps.shape[0], gated.shape[1]
    reach = count // 2
    padded = jnp.pad(gated, ((0, 0), (reach, reach), (0, 0)))
    total = padded[:, 0:length, :] * taps[0]
    for tap in range(1, count):
        total = total + padded[:, tap : tap + length, :] * taps[tap]
    return total.reshape(-1, width)


def attention_grads(rows, params, sequences, saved, grad):
    (
        gain,
        shift,
        query_w,
        query_b,
        key_w,
        value_w,
        value_b,
        place_w,
        content_b,
        place_b,
        output_w,
        output_b,
    ) = params
    normed, table, keys, values, places, query_u, query_v, mixing, mixing_low, context = saved
    width = rows.shape[1]
    length = rows.shape[0] // sequences
    depth = width // HEADS
    grad_low = rounded(grad)
    grad_output_w = product_left(context, grad_low)
    grad_output_b = jnp.sum(grad, axis=0)
    grad_context = rounded(product_right(grad_low, output_w)).reshape(
        sequences, length, HEADS, depth
    )
    grad_mixing = contract("slhd,smhd->shlm", grad_context, values)
    grad_values = contract("shlm,slhd->smhd", mixing_low, grad_context)
    grad_scores = (
        mixing
        * (grad_mixing - jnp.sum(mixing * grad_mixing, axis=-1, keepdims=True))
        * (1.0 / math.sqrt(depth))
    )
    scores_low = rounded(grad_scores)
    grad_query_u = contract("shlm,smhd->slhd", scores_low, keys)
    grad_keys = contract("shlm,slhd->smhd", scores_low, query_u)
    full_low = rounded(skew_back(grad_scores))
    grad_query_v = contract("shlk,khd->slhd", full_low, places)
    grad_places = contract("shlk,slhd->khd", full_low, query_v).reshape(2 * length, width)
    grad_place_w = jnp.dot(widened(table).T, grad_places, precision=lax.Precision.HIGHEST)
    grad_content_b = jnp.sum(grad_query_u, axis=(0, 1)).reshape(width)
    grad_place_b = jnp.sum(grad_query_v, axis=(0, 1)).reshape(width)
    grad_query = (grad_query_u + grad_query_v).reshape(rows.shape)
    grad_values = grad_values.reshape(rows.shape)
    query_low = rounded(grad_query)
    keys_low = rounded(grad_keys.reshape(rows.shape))
    values_low = rounded(grad_values)
    grad_query_w = product_left(normed, query_low)
    grad_query_b = jnp.sum(grad_query, axis=0)
    grad_key_w = product_left(normed, keys_low)
    grad_value_w = product_left(normed, values_low)
    grad_value_b = jnp.sum(grad_values, axis=0)
    grad_normed = (
        product_right(query_low, query_w)
        + product_right(keys_low, key_w)
        + product_right(values_low, value_w)
    )
    grad_rows, grad_gain, grad_shift = layer_norm_back(
        rows, widened(gain), widened(shift), grad_normed
    )
    grads = (
        grad_gain,
        grad_shift,
        grad_query_w,
        grad_query_b,
        grad_key_w,
        grad_value_w,
        grad_value_b,
        grad_place_w,
        grad_content_b,
        grad_place_b,
        grad_output_w,
        grad_output_b,
    )
    return (grad + grad_rows, grads)


def local_fast(inputs, *rest):
    params, cotangent = rest[:-1], rest[-1]
    (front_gain, front_shift, front_expand, front_lift, front_shrink, front_offset) = params[0:6]
    (
        attend_gain,
        attend_shift,
        query_w,
        query_b,
        key_w,
        value_w,
        value_b,
        place_w,
        content_b,
        place_b,
        output_w,
        output_b,
    ) = params[6:18]
    (
        module_gain,
        module_shift,
        gating_w,
        gating_b,
        depth_w,
        batch_gain,
        batch_shift,
        mixer_w,
        mixer_b,
    ) = params[18:27]
    (rear_gain, rear_shift, rear_expand, rear_lift, rear_shrink, rear_offset) = params[27:33]
    final_gain, final_shift = params[33:35]

    devices = lax.axis_size(AXIS)
    sequences, length, width = inputs.shape
    count = devices * sequences * length
    own = front_gain.shape[0]
    taps = depth_w.shape[1]
    index = lax.axis_index(AXIS)
    me = index.astype(jnp.int32).reshape(1)

    singles = jnp.stack(
        [
            front_gain, front_shift, front_offset,
            attend_gain, attend_shift, query_b, value_b, content_b, place_b, output_b,
            module_gain, module_shift, batch_gain, batch_shift, mixer_b,
            rear_gain, rear_shift, rear_offset, final_gain, final_shift,
        ],
        axis=0,
    )
    singles = jnp.pad(singles, ((0, 0), (0, 128 - own)))
    wide = [jnp.pad(v, (0, 128 - v.shape[0]))[None] for v in (front_lift, rear_lift, gating_b)]
    depth_rows = jnp.pad(depth_w.T, ((0, 2 * TILE_ROWS - taps), (0, 128 - own)))
    rows64 = jnp.concatenate(
        [singles] + wide + [jnp.zeros((2 * TILE_ROWS - 23, 128), singles.dtype), depth_rows], axis=0
    )
    vector_block = jnp.concatenate(
        [rows64[k * TILE_ROWS : (k + 1) * TILE_ROWS] for k in range(4)], axis=1
    )

    shapes = {
        "front_a": [front_expand.shape],
        "front_b": [front_shrink.shape],
        "middle_a": [gating_w.shape, query_w.shape, key_w.shape],
        "middle_b": [mixer_w.shape, value_w.shape, place_w.shape, output_w.shape],
        "rear_a": [rear_expand.shape],
        "rear_b": [rear_shrink.shape],
    }

    def stacked(*weights):
        return jnp.concatenate([piece for w in weights for piece in block_of(w, width)], axis=0)

    front_halves = gather_bundle(
        jnp.concatenate([stacked(front_expand), vector_block], axis=0), stacked(front_shrink), devices
    )
    middle_halves = gather_bundle(
        stacked(gating_w, query_w, key_w), stacked(mixer_w, value_w, place_w, output_w), devices
    )
    rear_halves = gather_bundle(stacked(rear_expand), stacked(rear_shrink), devices)

    front_expand, front_shrink, table, lifts, gates_bias = spread(
        me, front_halves, shapes["front_a"], shapes["front_b"], width, devices, stacked(params[2]).shape[0]
    )
    front = (table[0], table[1], front_expand, lifts[0], front_shrink, table[2])
    rows = widened(inputs).reshape(sequences * length, width)
    first, front_saved = feed_forward(rows, front)

    gating_w, query_w, key_w, mixer_w, value_w, place_w, output_w = spread(
        me, middle_halves, shapes["middle_a"], shapes["middle_b"], width, devices
    )
    attend = (
        table[3], table[4], query_w, table[5], key_w, value_w, table[6], place_w, table[7], table[8],
        output_w, table[9],
    )
    second, attend_saved = attention_parts(first, attend, sequences)

    module_gain, module_shift = table[10], table[11]
    depth_taps = table[2 * TILE_ROWS : 2 * TILE_ROWS + taps]
    normed2 = rounded(layer_norm(second, module_gain, module_shift))
    gates = product(normed2, gating_w) + gates_bias
    depth_out, depth_back = jax.vjp(partial(taps_depthwise, sequences=sequences), gates, depth_taps)
    sums = sum_all(
        jnp.stack([jnp.sum(depth_out, axis=0), jnp.sum(depth_out * depth_out, axis=0)], axis=0), devices
    )
    center = sums[0] / count
    inverse_root = lax.rsqrt(sums[1] / count - center * center + EPSILON)
    module_tail_params = (None,) * 5 + (table[12], table[13], mixer_w, table[14])
    third, tail_saved = module_tail(second, depth_out, module_tail_params, center, inverse_root)

    rear_expand, rear_shrink = spread(me, rear_halves, shapes["rear_a"], shapes["rear_b"], width, devices)
    rear = (table[15], table[16], rear_expand, lifts[1], rear_shrink, table[17])
    fourth, rear_saved = feed_forward(third, rear)
    closing_gain, closing_shift = table[18], table[19]
    outputs = layer_norm(fourth, closing_gain, closing_shift)
    grad_fourth, grad_final_gain, grad_final_shift = layer_norm_back(
        fourth, closing_gain, closing_shift, widened(cotangent).reshape(sequences * length, width)
    )
    grad_third, rear_grads = feed_forward_back(third, rear, rear_saved, grad_fourth)
    rear_done = reduce_bundle(
        collect(me, [rear_grads[2]], [rear_grads[4]], width, devices), devices
    )

    grad_normal, tail_grads = module_tail_back(module_tail_params, tail_saved, grad_third)
    normal = tail_saved[0]
    sums = sum_all(
        jnp.stack([jnp.sum(grad_normal, axis=0), jnp.sum(grad_normal * normal, axis=0)], axis=0), devices
    )
    grad_depth = inverse_root * (grad_normal - sums[0] / count - normal * (sums[1] / count))
    grad_gates, grad_taps = depth_back(grad_depth)
    gates_low = rounded(grad_gates)
    grad_gating_w = product_left(normed2, gates_low)
    grad_gating_b = jnp.sum(grad_gates, axis=0)
    grad_rows, grad_module_gain, grad_module_shift = layer_norm_back(
        second, module_gain, module_shift, product_right(gates_low, gating_w)
    )
    grad_second = grad_third + grad_rows
    late_rows = jnp.concatenate(
        [
            jnp.stack(
                [
                    grad_module_gain, grad_module_shift, tail_grads[0], tail_grads[1], tail_grads[3],
                    rear_grads[0], rear_grads[1], rear_grads[5], grad_final_gain, grad_final_shift,
                ],
                axis=0,
            ),
            rear_grads[3].reshape(4, width),
            grad_gating_b.reshape(2, width),
            grad_taps,
        ],
        axis=0,
    )
    late_sum = sum_all(late_rows, devices)

    grad_first, attend_grads = attention_grads(first, attend, sequences, attend_saved, grad_second)
    middle_done = reduce_bundle(
        collect(
            me,
            [grad_gating_w, attend_grads[2], attend_grads[4]],
            [tail_grads[2], attend_grads[5], attend_grads[7], attend_grads[10]],
            width,
            devices,
        ),
        devices,
    )
    grad_input, front_grads = feed_forward_back(rows, front, front_saved, grad_first)
    front_done = reduce_bundle(
        collect(me, [front_grads[2]], [front_grads[4]], width, devices), devices
    )
    early_rows = jnp.concatenate(
        [
            jnp.stack(
                [
                    front_grads[0], front_grads[1], front_grads[5],
                    attend_grads[0], attend_grads[1], attend_grads[3], attend_grads[6],
                    attend_grads[8], attend_grads[9], attend_grads[11],
                ],
                axis=0,
            ),
            front_grads[3].reshape(4, width),
        ],
        axis=0,
    )
    early_sum = sum_all(early_rows, devices)

    late_own = own_of(late_sum, index, own)
    early_own = own_of(early_sum, index, own)
    front_lift_own = lax.dynamic_slice(early_sum[10:14].reshape(-1), (index * 4 * own,), (4 * own,))
    rear_lift_own = lax.dynamic_slice(late_sum[10:14].reshape(-1), (index * 4 * own,), (4 * own,))
    gating_b_own = lax.dynamic_slice(late_sum[14:16].reshape(-1), (index * 2 * own,), (2 * own,))
    taps_own = late_own[16 : 16 + taps].T
    g_front_expand, g_front_shrink = shard_of(front_done, shapes["front_a"] + shapes["front_b"], width)
    g_gating, g_query, g_key, g_mixer, g_value, g_place, g_output = shard_of(
        middle_done, shapes["middle_a"] + shapes["middle_b"], width
    )
    g_rear_expand, g_rear_shrink = shard_of(rear_done, shapes["rear_a"] + shapes["rear_b"], width)
    e, l = early_own, late_own
    return (
        outputs.reshape(sequences, length, width),
        grad_input.reshape(sequences, length, width),
        e[0], e[1], g_front_expand, front_lift_own, g_front_shrink, e[2],
        e[3], e[4], g_query, e[5], g_key, g_value, e[6], g_place, e[7], e[8], g_output, e[9],
        l[0], l[1], g_gating, gating_b_own, taps_own, l[2], l[3], g_mixer, l[4],
        l[5], l[6], g_rear_expand, rear_lift_own, g_rear_shrink, l[7],
        l[8], l[9],
    )


def local(inputs, *rest):
    devices = lax.axis_size(AXIS)
    own = rest[0].shape[0]
    width = inputs.shape[2]
    taps = rest[22].shape[1]
    packs = own % TILE_ROWS == 0 and 4 * own <= 128 and width == 4 * 128 and taps <= 2 * TILE_ROWS
    if devices >= 8 and devices & (devices - 1) == 0 and packs:
        return local_fast(inputs, *rest)
    return local_plain(inputs, *rest)


def solution(mesh):
    placed = (
        P("fsdp", None, None),
        P("fsdp"),
        P("fsdp"),
        P("fsdp", None),
        P("fsdp"),
        P("fsdp", None),
        P("fsdp"),
        P("fsdp"),
        P("fsdp"),
        P("fsdp", None),
        P("fsdp"),
        P("fsdp", None),
        P("fsdp", None),
        P("fsdp"),
        P("fsdp", None),
        P("fsdp"),
        P("fsdp"),
        P("fsdp", None),
        P("fsdp"),
        P("fsdp"),
        P("fsdp"),
        P("fsdp", None),
        P("fsdp"),
        P("fsdp", None),
        P("fsdp"),
        P("fsdp"),
        P("fsdp", None),
        P("fsdp"),
        P("fsdp"),
        P("fsdp"),
        P("fsdp", None),
        P("fsdp"),
        P("fsdp", None),
        P("fsdp"),
        P("fsdp"),
        P("fsdp"),
        P("fsdp", None, None),
    )
    return jax.shard_map(
        local,
        mesh=mesh,
        in_specs=placed,
        out_specs=(
            P("fsdp", None, None),
            P("fsdp", None, None),
            P("fsdp"),
            P("fsdp"),
            P("fsdp", None),
            P("fsdp"),
            P("fsdp", None),
            P("fsdp"),
            P("fsdp"),
            P("fsdp"),
            P("fsdp", None),
            P("fsdp"),
            P("fsdp", None),
            P("fsdp", None),
            P("fsdp"),
            P("fsdp", None),
            P("fsdp"),
            P("fsdp"),
            P("fsdp", None),
            P("fsdp"),
            P("fsdp"),
            P("fsdp"),
            P("fsdp", None),
            P("fsdp"),
            P("fsdp", None),
            P("fsdp"),
            P("fsdp"),
            P("fsdp", None),
            P("fsdp"),
            P("fsdp"),
            P("fsdp"),
            P("fsdp", None),
            P("fsdp"),
            P("fsdp", None),
            P("fsdp"),
            P("fsdp"),
            P("fsdp"),
        ),
        check_vma=False,
    )
```

```python
from functools import partial
import math

import jax
import jax.numpy as jnp
from jax import lax
from jax.experimental import pallas as pl
from jax.experimental.pallas import tpu as pltpu
from jax.sharding import PartitionSpec as P

HEADS = 8


EPSILON = 1e-05


def rounded(value):
    return value.astype(jnp.bfloat16)


def widened(value):
    return value.astype(jnp.float32)


def product(left, right):
    return jnp.dot(left, right, preferred_element_type=jnp.float32)


def product_left(left, right):
    return jnp.dot(left.T, right, preferred_element_type=jnp.float32)


def product_right(left, right):
    return jnp.dot(left, right.T, preferred_element_type=jnp.float32)


def contract(form, left, right):
    return jnp.einsum(form, left, right, preferred_element_type=jnp.float32)


def layer_norm(rows, gain, shift):
    center = jnp.mean(rows, axis=-1, keepdims=True)
    spread = rows - center
    scale = lax.rsqrt(jnp.mean(spread * spread, axis=-1, keepdims=True) + EPSILON)
    return spread * scale * gain + shift


def layer_norm_back(rows, gain, shift, grad):
    _, pullback = jax.vjp(layer_norm, rows, gain, shift)
    return pullback(grad)


def swish(value):
    return value * jax.nn.sigmoid(value)


def swish_slope(value):
    sigma = jax.nn.sigmoid(value)
    return sigma * (1.0 + value * (1.0 - sigma))


def feed_forward(rows, params):
    gain, shift, expand, lift, shrink, offset = params
    normed = rounded(layer_norm(rows, widened(gain), widened(shift)))
    hidden = product(normed, expand) + widened(lift)
    active = rounded(swish(hidden))
    result = rows + 0.5 * (product(active, shrink) + widened(offset))
    return (result, (normed, hidden, active))


def feed_forward_back(rows, params, saved, grad):
    gain, shift, expand, lift, shrink, offset = params
    normed, hidden, active = saved
    half = 0.5 * grad
    half_low = rounded(half)
    grad_shrink = product_left(active, half_low)
    grad_offset = jnp.sum(half, axis=0)
    grad_hidden = product_right(half_low, shrink) * swish_slope(hidden)
    hidden_low = rounded(grad_hidden)
    grad_expand = product_left(normed, hidden_low)
    grad_lift = jnp.sum(grad_hidden, axis=0)
    grad_normed = product_right(hidden_low, expand)
    grad_rows, grad_gain, grad_shift = layer_norm_back(
        rows, widened(gain), widened(shift), grad_normed
    )
    return (
        grad + grad_rows,
        (grad_gain, grad_shift, grad_expand, grad_lift, grad_shrink, grad_offset),
    )


def place_table(length, width):
    distance = widened(length - 1 - jnp.arange(2 * length))
    rates = jnp.exp(widened(jnp.arange(width // 2)) * (-2.0 * math.log(10000.0) / width))
    angles = distance[:, None] * rates[None, :]
    return rounded(jnp.concatenate([jnp.sin(angles), jnp.cos(angles)], axis=1))


def skew(full):
    length = full.shape[-2]
    leading = full.shape[:-2]
    flat = full.reshape(leading + (2 * length * length,))
    flat = flat[..., length - 1 : length - 1 + length * (2 * length - 1)]
    return flat.reshape(leading + (length, 2 * length - 1))[..., :length]


def skew_back(grad_scores):
    sequences, heads, length, _ = grad_scores.shape
    base = jnp.zeros((sequences, heads, length, 2 * length), jnp.float32)
    _, pullback = jax.vjp(skew, base)
    return pullback(grad_scores)[0]


def attend_parts(rows, params, sequences):
    (
        gain,
        shift,
        query_w,
        query_b,
        key_w,
        value_w,
        value_b,
        place_w,
        content_b,
        place_b,
        output_w,
        output_b,
    ) = params
    width = rows.shape[1]
    length = rows.shape[0] // sequences
    depth = width // HEADS
    normed = rounded(layer_norm(rows, widened(gain), widened(shift)))
    query = product(normed, query_w) + widened(query_b)
    keys = rounded(product(normed, key_w)).reshape(sequences, length, HEADS, depth)
    values = rounded(product(normed, value_w) + widened(value_b)).reshape(
        sequences, length, HEADS, depth
    )
    table = place_table(length, width)
    places = rounded(product(table, place_w)).reshape(2 * length, HEADS, depth)
    query_u = rounded(query + widened(content_b)).reshape(sequences, length, HEADS, depth)
    query_v = rounded(query + widened(place_b)).reshape(sequences, length, HEADS, depth)
    content = contract("slhd,smhd->shlm", query_u, keys)
    positional = skew(contract("slhd,khd->shlk", query_v, places))
    scores = (content + positional) * (1.0 / math.sqrt(depth))
    return (normed, table, keys, values, places, query_u, query_v, scores)


def attention(rows, params, sequences):
    output_w, output_b = (params[10], params[11])
    parts = attend_parts(rows, params, sequences)
    values, scores = (parts[3], parts[7])
    total = jnp.log(jnp.sum(jnp.exp(scores), axis=-1))
    mixing = rounded(jnp.exp(scores - total[..., None]))
    context = rounded(contract("shlm,smhd->slhd", mixing, values).reshape(rows.shape))
    return (rows + product(context, output_w) + widened(output_b), total)


def attention_back(rows, params, sequences, total, grad):
    (
        gain,
        shift,
        query_w,
        query_b,
        key_w,
        value_w,
        value_b,
        place_w,
        content_b,
        place_b,
        output_w,
        output_b,
    ) = params
    normed, table, keys, values, places, query_u, query_v, scores = attend_parts(
        rows, params, sequences
    )
    width = rows.shape[1]
    length = rows.shape[0] // sequences
    depth = width // HEADS
    mixing = jnp.exp(scores - total[..., None])
    mixing_low = rounded(mixing)
    context = rounded(contract("shlm,smhd->slhd", mixing_low, values).reshape(rows.shape))
    grad_low = rounded(grad)
    grad_output_w = product_left(context, grad_low)
    grad_output_b = jnp.sum(grad, axis=0)
    grad_context = rounded(product_right(grad_low, output_w)).reshape(
        sequences, length, HEADS, depth
    )
    grad_mixing = contract("slhd,smhd->shlm", grad_context, values)
    grad_values = contract("shlm,slhd->smhd", mixing_low, grad_context)
    grad_scores = (
        mixing
        * (grad_mixing - jnp.sum(mixing * grad_mixing, axis=-1, keepdims=True))
        * (1.0 / math.sqrt(depth))
    )
    scores_low = rounded(grad_scores)
    grad_query_u = contract("shlm,smhd->slhd", scores_low, keys)
    grad_keys = contract("shlm,slhd->smhd", scores_low, query_u)
    full_low = rounded(skew_back(grad_scores))
    grad_query_v = contract("shlk,khd->slhd", full_low, places)
    grad_places = contract("shlk,slhd->khd", full_low, query_v).reshape(2 * length, width)
    grad_place_w = jnp.dot(widened(table).T, grad_places, precision=lax.Precision.HIGHEST)
    grad_content_b = jnp.sum(grad_query_u, axis=(0, 1)).reshape(width)
    grad_place_b = jnp.sum(grad_query_v, axis=(0, 1)).reshape(width)
    grad_query = (grad_query_u + grad_query_v).reshape(rows.shape)
    grad_values = grad_values.reshape(rows.shape)
    query_low = rounded(grad_query)
    keys_low = rounded(grad_keys.reshape(rows.shape))
    values_low = rounded(grad_values)
    grad_query_w = product_left(normed, query_low)
    grad_query_b = jnp.sum(grad_query, axis=0)
    grad_key_w = product_left(normed, keys_low)
    grad_value_w = product_left(normed, values_low)
    grad_value_b = jnp.sum(grad_values, axis=0)
    grad_normed = (
        product_right(query_low, query_w)
        + product_right(keys_low, key_w)
        + product_right(values_low, value_w)
    )
    grad_rows, grad_gain, grad_shift = layer_norm_back(
        rows, widened(gain), widened(shift), grad_normed
    )
    grads = (
        grad_gain,
        grad_shift,
        grad_query_w,
        grad_query_b,
        grad_key_w,
        grad_value_w,
        grad_value_b,
        grad_place_w,
        grad_content_b,
        grad_place_b,
        grad_output_w,
        grad_output_b,
    )
    return (grad + grad_rows, grads)


def depthwise(signal, kernel):
    taps = kernel.shape[1]
    reach = taps // 2
    length = signal.shape[1]
    padded = jnp.pad(signal, ((0, 0), (reach, reach), (0, 0)))
    total = padded[:, 0:length, :] * kernel[:, 0]
    for tap in range(1, taps):
        total = total + padded[:, tap : tap + length, :] * kernel[:, tap]
    return total


def gated_depthwise(gates, kernel, sequences):
    width = kernel.shape[0]
    gated = gates[:, :width] * jax.nn.sigmoid(gates[:, width:])
    return depthwise(gated.reshape(sequences, -1, width), kernel).reshape(-1, width)


def module_head(rows, params, sequences):
    gain, shift, gating_w, gating_b, depth_w = params[:5]
    normed = rounded(layer_norm(rows, widened(gain), widened(shift)))
    gates = product(normed, gating_w) + widened(gating_b)
    return (normed, gates, gated_depthwise(gates, widened(depth_w), sequences))


def module_head_back(rows, params, sequences, grad_depth, grad):
    gain, shift, gating_w, gating_b, depth_w = params[:5]
    normed = rounded(layer_norm(rows, widened(gain), widened(shift)))
    gates = product(normed, gating_w) + widened(gating_b)
    _, pullback = jax.vjp(partial(gated_depthwise, sequences=sequences), gates, widened(depth_w))
    grad_gates, grad_kernel = pullback(grad_depth)
    gates_low = rounded(grad_gates)
    grad_gating_w = product_left(normed, gates_low)
    grad_gating_b = jnp.sum(grad_gates, axis=0)
    grad_normed = product_right(gates_low, gating_w)
    grad_rows, grad_gain, grad_shift = layer_norm_back(
        rows, widened(gain), widened(shift), grad_normed
    )
    return (grad + grad_rows, (grad_gain, grad_shift, grad_gating_w, grad_gating_b, grad_kernel))


def module_tail(rows, depth_out, params, center, inverse_root):
    batch_gain, batch_shift, mixer_w, mixer_b = params[5:]
    normal = (depth_out - center) * inverse_root
    batch_out = normal * widened(batch_gain) + widened(batch_shift)
    activated = rounded(swish(batch_out))
    return (rows + product(activated, mixer_w) + widened(mixer_b), (normal, batch_out, activated))


def module_tail_back(params, saved, grad):
    batch_gain, batch_shift, mixer_w, mixer_b = params[5:]
    normal, batch_out, activated = saved
    grad_low = rounded(grad)
    grad_mixer_w = product_left(activated, grad_low)
    grad_mixer_b = jnp.sum(grad, axis=0)
    grad_batch = product_right(grad_low, mixer_w) * swish_slope(batch_out)
    grad_batch_gain = jnp.sum(grad_batch * normal, axis=0)
    grad_batch_shift = jnp.sum(grad_batch, axis=0)
    grad_normal = grad_batch * widened(batch_gain)
    return (grad_normal, (grad_batch_gain, grad_batch_shift, grad_mixer_w, grad_mixer_b))


def pack_early(front, attend):
    vectors = jnp.stack(
        [
            front[0],
            front[1],
            front[5],
            attend[0],
            attend[1],
            attend[3],
            attend[6],
            attend[8],
            attend[9],
            attend[11],
        ],
        axis=0,
    )
    joined = jnp.concatenate([attend[2], attend[4], attend[5], attend[7], attend[10]], axis=1)
    return (vectors, front[3], front[2], front[4], joined)


def unpack_early(packed):
    vectors, lift, expand, shrink, joined = packed
    span = joined.shape[1] // 5
    front = (vectors[0], vectors[1], expand, lift, shrink, vectors[2])
    attend = (
        vectors[3],
        vectors[4],
        joined[:, 0:span],
        vectors[5],
        joined[:, span : 2 * span],
        joined[:, 2 * span : 3 * span],
        vectors[6],
        joined[:, 3 * span : 4 * span],
        vectors[7],
        vectors[8],
        joined[:, 4 * span : 5 * span],
        vectors[9],
    )
    return (front, attend)


def pack_module(module):
    vectors = jnp.stack([module[0], module[1], module[5], module[6], module[8]], axis=0)
    joined = jnp.concatenate([module[2], module[7]], axis=1)
    return (vectors, module[3], joined, module[4])


def unpack_module(packed):
    vectors, gating_b, joined, kernel = packed
    span = joined.shape[1] // 3
    return (
        vectors[0],
        vectors[1],
        joined[:, 0 : 2 * span],
        gating_b,
        kernel,
        vectors[2],
        vectors[3],
        joined[:, 2 * span : 3 * span],
        vectors[4],
    )


def pack_rear(rear, closing):
    vectors = jnp.stack([rear[0], rear[1], rear[5], closing[0], closing[1]], axis=0)
    return (vectors, rear[3], rear[2], rear[4])


def unpack_rear(packed):
    vectors, lift, expand, shrink = packed
    return ((vectors[0], vectors[1], expand, lift, shrink, vectors[2]), (vectors[3], vectors[4]))


def local_plain(
    inputs,
    front_gain,
    front_shift,
    front_expand,
    front_lift,
    front_shrink,
    front_offset,
    attend_gain,
    attend_shift,
    query_weight,
    query_bias,
    key_weight,
    value_weight,
    value_bias,
    place_weight,
    content_bias,
    place_bias,
    output_weight,
    output_bias,
    module_gain,
    module_shift,
    gating_weight,
    gating_bias,
    depth_weight,
    batch_gain,
    batch_shift,
    mixer_weight,
    mixer_bias,
    rear_gain,
    rear_shift,
    rear_expand,
    rear_lift,
    rear_shrink,
    rear_offset,
    final_gain,
    final_shift,
    cotangent,
):
    sequences, length, width = inputs.shape
    count = lax.axis_size("fsdp") * sequences * length
    rows = widened(inputs).reshape(sequences * length, width)
    front_own = (front_gain, front_shift, front_expand, front_lift, front_shrink, front_offset)
    attend_own = (
        attend_gain,
        attend_shift,
        query_weight,
        query_bias,
        key_weight,
        value_weight,
        value_bias,
        place_weight,
        content_bias,
        place_bias,
        output_weight,
        output_bias,
    )
    module_own = (
        module_gain,
        module_shift,
        gating_weight,
        gating_bias,
        depth_weight,
        batch_gain,
        batch_shift,
        mixer_weight,
        mixer_bias,
    )
    rear_own = (rear_gain, rear_shift, rear_expand, rear_lift, rear_shrink, rear_offset)
    early_own = pack_early(front_own, attend_own)
    early = (
        lax.all_gather(early_own[0], "fsdp", axis=1, tiled=True),
        lax.all_gather(early_own[1], "fsdp", axis=0, tiled=True),
        lax.all_gather(early_own[2], "fsdp", axis=0, tiled=True),
        lax.all_gather(early_own[3], "fsdp", axis=0, tiled=True),
        lax.all_gather(early_own[4], "fsdp", axis=0, tiled=True),
    )
    front, attend = unpack_early(early)
    first = feed_forward(rows, front)[0]
    module_pack = pack_module(module_own)
    rear_pack = pack_rear(rear_own, (final_gain, final_shift))
    late = (
        lax.all_gather(module_pack[0], "fsdp", axis=1, tiled=True),
        lax.all_gather(module_pack[1], "fsdp", axis=0, tiled=True),
        lax.all_gather(module_pack[2], "fsdp", axis=0, tiled=True),
        lax.all_gather(module_pack[3], "fsdp", axis=0, tiled=True),
        lax.all_gather(rear_pack[0], "fsdp", axis=1, tiled=True),
        lax.all_gather(rear_pack[1], "fsdp", axis=0, tiled=True),
        lax.all_gather(rear_pack[2], "fsdp", axis=0, tiled=True),
        lax.all_gather(rear_pack[3], "fsdp", axis=0, tiled=True),
    )
    second, total = attention(first, attend, sequences)
    module = unpack_module(late[0:4])
    rear, closing = unpack_rear(late[4:8])
    depth_out = module_head(second, module, sequences)[2]
    first_sum, square_sum = lax.psum(
        (jnp.sum(depth_out, axis=0), jnp.sum(depth_out * depth_out, axis=0)), "fsdp"
    )
    center = first_sum / count
    inverse_root = lax.rsqrt(square_sum / count - center * center + EPSILON)
    third, tail_saved = module_tail(second, depth_out, module, center, inverse_root)
    fourth, rear_saved = feed_forward(third, rear)
    closing_gain, closing_shift = (widened(closing[0]), widened(closing[1]))
    outputs = layer_norm(fourth, closing_gain, closing_shift)
    grad_fourth, grad_final_gain, grad_final_shift = layer_norm_back(
        fourth, closing_gain, closing_shift, widened(cotangent).reshape(sequences * length, width)
    )
    grad_third, rear_grads = feed_forward_back(third, rear, rear_saved, grad_fourth)
    again = (
        lax.all_gather(early_own[0], "fsdp", axis=1, tiled=True),
        lax.all_gather(early_own[1], "fsdp", axis=0, tiled=True),
        lax.all_gather(early_own[2], "fsdp", axis=0, tiled=True),
        lax.all_gather(early_own[3], "fsdp", axis=0, tiled=True),
        lax.all_gather(early_own[4], "fsdp", axis=0, tiled=True),
        lax.all_gather(module_pack[0], "fsdp", axis=1, tiled=True),
        lax.all_gather(module_pack[1], "fsdp", axis=0, tiled=True),
        lax.all_gather(module_pack[2], "fsdp", axis=0, tiled=True),
        lax.all_gather(module_pack[3], "fsdp", axis=0, tiled=True),
    )
    front_again, attend_again = unpack_early(again[0:5])
    module_again = unpack_module(again[5:9])
    grad_normal, tail_grads = module_tail_back(module_again, tail_saved, grad_third)
    normal = tail_saved[0]
    normal_sum, cross_sum = lax.psum(
        (jnp.sum(grad_normal, axis=0), jnp.sum(grad_normal * normal, axis=0)), "fsdp"
    )
    grad_depth = inverse_root * (grad_normal - normal_sum / count - normal * (cross_sum / count))
    grad_second, head_grads = module_head_back(
        second, module_again, sequences, grad_depth, grad_third
    )
    module_all = head_grads + tail_grads
    late_grad_pack = pack_module(module_all) + pack_rear(
        rear_grads, (grad_final_gain, grad_final_shift)
    )
    late_done = (
        lax.psum_scatter(late_grad_pack[0], "fsdp", scatter_dimension=1, tiled=True),
        lax.psum_scatter(late_grad_pack[1], "fsdp", scatter_dimension=0, tiled=True),
        lax.psum_scatter(late_grad_pack[2], "fsdp", scatter_dimension=0, tiled=True),
        lax.psum_scatter(late_grad_pack[3], "fsdp", scatter_dimension=0, tiled=True),
        lax.psum_scatter(late_grad_pack[4], "fsdp", scatter_dimension=1, tiled=True),
        lax.psum_scatter(late_grad_pack[5], "fsdp", scatter_dimension=0, tiled=True),
        lax.psum_scatter(late_grad_pack[6], "fsdp", scatter_dimension=0, tiled=True),
        lax.psum_scatter(late_grad_pack[7], "fsdp", scatter_dimension=0, tiled=True),
    )
    grad_first, attend_all = attention_back(first, attend_again, sequences, total, grad_second)
    grad_input, front_all = feed_forward_back(
        rows, front_again, feed_forward(rows, front_again)[1], grad_first
    )
    early_grad_pack = pack_early(front_all, attend_all)
    early_done = (
        lax.psum_scatter(early_grad_pack[0], "fsdp", scatter_dimension=1, tiled=True),
        lax.psum_scatter(early_grad_pack[1], "fsdp", scatter_dimension=0, tiled=True),
        lax.psum_scatter(early_grad_pack[2], "fsdp", scatter_dimension=0, tiled=True),
        lax.psum_scatter(early_grad_pack[3], "fsdp", scatter_dimension=0, tiled=True),
        lax.psum_scatter(early_grad_pack[4], "fsdp", scatter_dimension=0, tiled=True),
    )
    front_out, attend_out = unpack_early(early_done)
    module_out = unpack_module(late_done[0:4])
    rear_out, closing_out = unpack_rear(late_done[4:8])
    return (
        (outputs.reshape(sequences, length, width), grad_input.reshape(sequences, length, width))
        + tuple(front_out)
        + tuple(attend_out)
        + tuple(module_out)
        + tuple(rear_out)
        + tuple(closing_out)
    )


AXIS = "fsdp"
TILE_ROWS = 16


def swap(value, bit, devices):
    return lax.ppermute(value, AXIS, [(i, i ^ bit) for i in range(devices)])


def stage_orders(devices):
    order = []
    bit = devices // 2
    while bit >= 1:
        order.append(bit)
        bit //= 2
    other = list(order)
    other[-3], other[-2] = other[-2], other[-3]
    return order, other


def relative(position, order):
    total = 0
    for place, bit in enumerate(order[:-1]):
        if (position >> place) & 1:
            total ^= bit
    return total


def tie(*groups):
    return lax.optimization_barrier(groups)


class Gather:
    def __init__(self, block_a, block_b, devices):
        self.devices = devices
        self.order_a, self.order_b = stage_orders(devices)
        self.heads = len(self.order_a) - 3
        self.split = block_a.shape[0]
        self.stage = 0
        self.state = (jnp.concatenate([block_a, block_b], axis=0)[None],)

    def advance(self):
        stage, self.stage = self.stage, self.stage + 1
        if stage < self.heads:
            (both,) = self.state
            both = jnp.concatenate([both, swap(both, self.order_a[stage], self.devices)], axis=0)
            self.state = (both,)
            if stage == self.heads - 1:
                self.state = (both[:, : self.split], both[:, self.split :])
            return
        part_a, part_b = self.state
        next_a = swap(part_a, self.order_a[stage], self.devices)
        next_b = swap(part_b, self.order_b[stage], self.devices)
        if stage == len(self.order_a) - 1:
            self.state = (part_a, next_a, part_b, next_b)
        else:
            self.state = (
                jnp.concatenate([part_a, next_a], axis=0),
                jnp.concatenate([part_b, next_b], axis=0),
            )


class Reduce:
    def __init__(self, halves, devices):
        self.devices = devices
        self.order_a, self.order_b = stage_orders(devices)
        self.heads = len(self.order_a) - 3
        keep_a, send_a, keep_b, send_b = halves
        self.stage = len(self.order_a) - 2
        self.state = (keep_a, swap(send_a, 1, devices), keep_b, swap(send_b, 1, devices))

    def step(self, keep, got, bit):
        half = keep.shape[0] // 2
        send = rounded(widened(keep[half:]) + widened(got[half:]))
        arrived = swap(send, bit, self.devices)
        return rounded(widened(keep[:half]) + widened(got[:half])), arrived

    def advance(self):
        stage, self.stage = self.stage, self.stage - 1
        if stage >= self.heads:
            keep_a, got_a, keep_b, got_b = self.state
            self.state = self.step(keep_a, got_a, self.order_a[stage]) + self.step(
                keep_b, got_b, self.order_b[stage]
            )
            return
        if stage == self.heads - 1:
            keep_a, got_a, keep_b, got_b = self.state
            self.state = (
                jnp.concatenate([keep_a, keep_b], axis=1),
                jnp.concatenate([got_a, got_b], axis=1),
            )
        self.state = self.step(*self.state, self.order_a[stage])

    def result(self):
        keep, got = self.state
        return (widened(keep) + widened(got))[0]


class Sum:
    def __init__(self, value, devices):
        order = stage_orders(devices)[0]
        heads = len(order) - 3
        self.bits = order[heads:] + order[:heads][::-1]
        self.devices = devices
        self.stage = 0
        self.state = (value,)

    def advance(self, stages=1):
        for _ in range(stages):
            (value,) = self.state
            self.state = (value + swap(value, self.bits[self.stage], self.devices),)
            self.stage += 1

    def finish(self):
        self.advance(len(self.bits) - self.stage)
        return self.state[0]


def tie_stages(*members):
    states = lax.optimization_barrier(tuple(m.state for m in members))
    for member, state in zip(members, states):
        member.state = state


def block_of(weight, width):
    blocks = weight.shape[1] // width
    return [weight[:, k * width : (k + 1) * width] for k in range(blocks)]


def plan_of(shapes, width):
    plan, offset = [], 0
    for rows, columns in shapes:
        blocks = columns // width
        plan.append((rows, blocks, offset))
        offset += rows * blocks
    return plan


def spread_kernel(devices, width, plans, vector, me_ref, *refs):
    halves, outs = refs[:4], refs[4:]
    orders = stage_orders(devices)
    me = me_ref[0]
    for colour in range(2):
        base = colour * len(plans[0])
        for core in range(2):
            source = halves[2 * colour + core]
            for position in range(devices // 2):
                owner = me ^ (relative(position, orders[colour]) ^ core)
                for item, (rows, blocks, offset) in enumerate(plans[colour]):
                    start = pl.multiple_of(owner * rows, rows)
                    for k in range(blocks):
                        outs[base + item][pl.ds(start, rows), k * width : (k + 1) * width] = source[
                            position, offset + k * rows : offset + (k + 1) * rows, :
                        ]
                if vector is not None and colour == 0:
                    start = pl.multiple_of(owner * TILE_ROWS, TILE_ROWS)
                    refs[-1][pl.ds(start, TILE_ROWS), :] = source[position, vector : vector + TILE_ROWS, :]
    if vector is not None:
        table, lifts, bias, held = refs[-4:]
        own = width // devices
        groups = width // 128
        for owner in range(devices):
            tile = widened(held[owner * TILE_ROWS : (owner + 1) * TILE_ROWS, :])
            for k in range(groups):
                table[k * TILE_ROWS : (k + 1) * TILE_ROWS, owner * own : (owner + 1) * own] = tile[
                    :, k * 128 : k * 128 + own
                ]
            lifts[:, owner * 4 * own : (owner + 1) * 4 * own] = tile[4:6, 128 : 128 + 4 * own]
            bias[:, owner * 2 * own : (owner + 1) * 2 * own] = tile[6:7, 128 : 128 + 2 * own]


def spread(me, halves, shapes_a, shapes_b, width, devices, vector=None):
    plans = (plan_of(shapes_a, width), plan_of(shapes_b, width))
    out_shape = [
        jax.ShapeDtypeStruct((devices * rows, columns), jnp.bfloat16) for rows, columns in shapes_a + shapes_b
    ]
    scratch = []
    if vector is not None:
        out_shape += [
            jax.ShapeDtypeStruct((width // 128 * TILE_ROWS, width), jnp.float32),
            jax.ShapeDtypeStruct((2, 4 * width), jnp.float32),
            jax.ShapeDtypeStruct((1, 2 * width), jnp.float32),
        ]
        scratch = [pltpu.VMEM((devices * TILE_ROWS, width), jnp.bfloat16)]
    return pl.pallas_call(
        partial(spread_kernel, devices, width, plans, vector),
        out_shape=out_shape,
        in_specs=[pl.BlockSpec(memory_space=pltpu.SMEM)] + [pl.BlockSpec(memory_space=pltpu.VMEM)] * 4,
        out_specs=[pl.BlockSpec(memory_space=pltpu.VMEM)] * len(out_shape),
        scratch_shapes=scratch,
        name="spread",
    )(me, *halves)


def across(left, right):
    return lax.dot_general(left, right, (((0,), (0,)), ((), ())), preferred_element_type=jnp.float32)


def against(left, right):
    return lax.dot_general(left, right, (((1,), (1,)), ((), ())), preferred_element_type=jnp.float32)


def total_of(value):
    return jnp.sum(value, axis=0, keepdims=True)


def norm_back(rows, gain, grad):
    center = jnp.mean(rows, axis=-1, keepdims=True)
    spread_rows = rows - center
    scale = lax.rsqrt(jnp.mean(spread_rows * spread_rows, axis=-1, keepdims=True) + EPSILON)
    normal = spread_rows * scale
    scaled = grad * gain
    pulled = scale * (
        scaled
        - jnp.mean(scaled, axis=-1, keepdims=True)
        - normal * jnp.mean(scaled * normal, axis=-1, keepdims=True)
    )
    return pulled, total_of(grad * normal), total_of(grad)


def row_of(table, index):
    return table[index : index + 1, :]


def whole(kernel, out_shape, operands, scratch=(), name=None, first_smem=False):
    space = pl.BlockSpec(memory_space=pltpu.VMEM)
    in_specs = [space] * len(operands)
    if first_smem:
        in_specs[0] = pl.BlockSpec(memory_space=pltpu.SMEM)
    return pl.pallas_call(
        kernel,
        out_shape=[jax.ShapeDtypeStruct(s, d) for s, d in out_shape],
        in_specs=in_specs,
        out_specs=[space] * len(out_shape),
        scratch_shapes=list(scratch),
        name=name,
    )(*operands)


F32, BF16 = jnp.float32, jnp.bfloat16


def front_kernel(rows_ref, table_ref, lifts_ref, expand_ref, shrink_ref, first_ref, normed_ref, hidden_ref, active_ref):
    rows = widened(rows_ref[...])
    normed = rounded(layer_norm(rows, row_of(table_ref, 0), row_of(table_ref, 1)))
    hidden = product(normed, expand_ref[...]) + lifts_ref[0:1, :]
    active = rounded(swish(hidden))
    first_ref[...] = rows + 0.5 * (product(active, shrink_ref[...]) + row_of(table_ref, 2))
    normed_ref[...] = normed
    hidden_ref[...] = hidden
    active_ref[...] = active


def attention_kernel(
    taps,
    first_ref, places_ref, table_ref, bias_ref, query_ref, key_ref, value_ref, output_ref, gating_ref,
    second_ref, normed1_ref, keys_ref, values_ref, query_u_ref, query_v_ref, mixing_ref, context_ref,
    normed2_ref, gates_ref, depth_ref, stats_ref,
    held,
):
    first = first_ref[...]
    length, width = first.shape
    depth = width // HEADS
    normed = rounded(layer_norm(first, row_of(table_ref, 3), row_of(table_ref, 4)))
    normed1_ref[...] = normed
    query = product(normed, query_ref[...]) + row_of(table_ref, 5)
    keys_ref[...] = rounded(product(normed, key_ref[...]))
    values_ref[...] = rounded(product(normed, value_ref[...]) + row_of(table_ref, 6))
    query_u_ref[...] = rounded(query + row_of(table_ref, 7))
    query_v_ref[...] = rounded(query + row_of(table_ref, 8))
    lane = lax.broadcasted_iota(jnp.int32, (length, 2 * depth), 1)
    for pair in range(HEADS // 2):
        columns = slice(pair * 2 * depth, (pair + 1) * 2 * depth)
        keys, values, places = keys_ref[:, columns], values_ref[:, columns], places_ref[:, columns]
        both = None
        for side in range(2):
            mine = (lane < depth) if side == 0 else (lane >= depth)
            query_u = jnp.where(mine, query_u_ref[:, columns], jnp.zeros((), BF16))
            query_v = jnp.where(mine, query_v_ref[:, columns], jnp.zeros((), BF16))
            full = against(query_v, places)
            positional = pltpu.roll(full, length + 1, 1, stride=1, stride_axis=0)[:, :length]
            scores = (against(query_u, keys) + positional) * (1.0 / math.sqrt(depth))
            total = jnp.log(jnp.sum(jnp.exp(scores), axis=-1, keepdims=True))
            mixing = jnp.exp(scores - total)
            mixing_ref[2 * pair + side] = mixing
            part = product(rounded(mixing), values)
            both = part if side == 0 else jnp.where(mine, part, both)
        context_ref[:, columns] = rounded(both)
    second = first + product(context_ref[...], output_ref[...]) + row_of(table_ref, 9)
    second_ref[...] = second
    normed2 = rounded(layer_norm(second, row_of(table_ref, 10), row_of(table_ref, 11)))
    normed2_ref[...] = normed2
    gates = product(normed2, gating_ref[...]) + bias_ref[...]
    gates_ref[...] = gates
    gated = gates[:, :width] * jax.nn.sigmoid(gates[:, width:])
    depth_out = taps_sum(held, gated, table_ref, taps, False)
    depth_ref[...] = depth_out
    stats_ref[0:1, :] = total_of(depth_out)
    stats_ref[1:2, :] = total_of(depth_out * depth_out)


def taps_sum(held, value, table_ref, taps, reverse):
    length = value.shape[0]
    margin = TILE_ROWS
    reach = taps // 2
    held[0:margin, :] = jnp.zeros_like(held[0:margin, :])
    held[margin + length :, :] = jnp.zeros_like(held[margin + length :, :])
    held[margin : margin + length, :] = value
    total = None
    for tap in range(taps):
        start = margin + (reach - tap if reverse else tap - reach)
        term = held[start : start + length, :] * row_of(table_ref, 2 * TILE_ROWS + tap)
        total = term if total is None else total + term
    return total


def rear_kernel(
    count,
    second_ref, depth_ref, sums_ref, table_ref, lifts_ref, mixer_ref, expand_ref, shrink_ref, cotangent_ref,
    outputs_ref, third_grad_ref, normal_grad_ref, normal_ref, stats_ref, vectors_ref, lift_ref,
    normed_ref, hidden_low_ref, active_ref, half_ref, activated_ref, third_low_ref,
):
    center = sums_ref[0:1, :] * (1.0 / count)
    inverse_root = lax.rsqrt(sums_ref[1:2, :] * (1.0 / count) - center * center + EPSILON)
    normal = (depth_ref[...] - center) * inverse_root
    normal_ref[...] = normal
    batch_gain, batch_shift = row_of(table_ref, 12), row_of(table_ref, 13)
    batch_out = normal * batch_gain + batch_shift
    activated = rounded(swish(batch_out))
    activated_ref[...] = activated
    third = second_ref[...] + product(activated, mixer_ref[...]) + row_of(table_ref, 14)
    normed = rounded(layer_norm(third, row_of(table_ref, 15), row_of(table_ref, 16)))
    normed_ref[...] = normed
    hidden = product(normed, expand_ref[...]) + lifts_ref[1:2, :]
    active = rounded(swish(hidden))
    active_ref[...] = active
    fourth = third + 0.5 * (product(active, shrink_ref[...]) + row_of(table_ref, 17))
    outputs_ref[...] = layer_norm(fourth, row_of(table_ref, 18), row_of(table_ref, 19))
    grad, gain_grad, shift_grad = norm_back(fourth, row_of(table_ref, 18), widened(cotangent_ref[...]))
    vectors_ref[8:9, :] = gain_grad
    vectors_ref[9:10, :] = shift_grad
    half = 0.5 * grad
    half_low = rounded(half)
    half_ref[...] = half_low
    vectors_ref[7:8, :] = total_of(half)
    grad_hidden = against(half_low, shrink_ref[...]) * swish_slope(hidden)
    lift_ref[...] = total_of(grad_hidden)
    hidden_low = rounded(grad_hidden)
    hidden_low_ref[...] = hidden_low
    pulled, gain_grad, shift_grad = norm_back(third, row_of(table_ref, 15), against(hidden_low, expand_ref[...]))
    vectors_ref[5:6, :] = gain_grad
    vectors_ref[6:7, :] = shift_grad
    third_grad = grad + pulled
    third_grad_ref[...] = third_grad
    third_low = rounded(third_grad)
    third_low_ref[...] = third_low
    vectors_ref[4:5, :] = total_of(third_grad)
    batch_grad = against(third_low, mixer_ref[...]) * swish_slope(batch_out)
    vectors_ref[2:3, :] = total_of(batch_grad * normal)
    vectors_ref[3:4, :] = total_of(batch_grad)
    normal_grad = batch_grad * batch_gain
    normal_grad_ref[...] = normal_grad
    stats_ref[0:1, :] = total_of(normal_grad)
    stats_ref[1:2, :] = total_of(normal_grad * normal)


def module_back_kernel(
    count, taps,
    third_grad_ref, normal_grad_ref, normal_ref, sums_ref, sums2_ref, table_ref, gates_ref, second_ref, gating_ref,
    second_grad_ref, second_low_ref, gates_low_ref, vectors_ref, bias_ref, taps_ref,
    held, other,
):
    length, width = normal_ref.shape
    center = sums_ref[0:1, :] * (1.0 / count)
    inverse_root = lax.rsqrt(sums_ref[1:2, :] * (1.0 / count) - center * center + EPSILON)
    depth_grad = inverse_root * (
        normal_grad_ref[...] - sums2_ref[0:1, :] * (1.0 / count) - normal_ref[...] * (sums2_ref[1:2, :] * (1.0 / count))
    )
    gated_grad = taps_sum(held, depth_grad, table_ref, taps, True)
    sigma = jax.nn.sigmoid(gates_ref[:, width:])
    values = gates_ref[:, :width]
    margin = TILE_ROWS
    other[0:margin, :] = jnp.zeros_like(other[0:margin, :])
    other[margin + length :, :] = jnp.zeros_like(other[margin + length :, :])
    other[margin : margin + length, :] = values * sigma
    for tap in range(taps):
        start = margin + tap - taps // 2
        taps_ref[tap : tap + 1, :] = total_of(other[start : start + length, :] * held[margin : margin + length, :])
    value_grad = gated_grad * sigma
    sigma_grad = gated_grad * values * sigma * (1.0 - sigma)
    bias_ref[:, :width] = total_of(value_grad)
    bias_ref[:, width:] = total_of(sigma_grad)
    gates_low_ref[:, :width] = rounded(value_grad)
    gates_low_ref[:, width:] = rounded(sigma_grad)
    pulled, gain_grad, shift_grad = norm_back(
        second_ref[...], row_of(table_ref, 10), against(gates_low_ref[...], gating_ref[...])
    )
    vectors_ref[0:1, :] = gain_grad
    vectors_ref[1:2, :] = shift_grad
    second_grad = third_grad_ref[...] + pulled
    second_grad_ref[...] = second_grad
    second_low_ref[...] = rounded(second_grad)


def attention_back_kernel(
    second_grad_ref, second_low_ref, first_ref, table_ref, places_ref, keys_ref, values_ref, query_u_ref,
    query_v_ref, mixing_ref, output_ref, query_w_ref, key_w_ref, value_w_ref,
    first_grad_ref, query_low_ref, keys_low_ref, values_low_ref, places_grad_ref, vectors_ref,
    scores, context_grad, wide_scores, grad_u, grad_v,
):
    length, width = first_ref.shape
    depth = width // HEADS
    vectors_ref[9:10, :] = total_of(second_grad_ref[...])
    context_grad[...] = rounded(against(second_low_ref[...], output_ref[...]))
    lane = lax.broadcasted_iota(jnp.int32, (length, 2 * depth), 1)
    near = lax.broadcasted_iota(jnp.int32, (length, length), 0)
    far = lax.broadcasted_iota(jnp.int32, (length, length), 1)
    flip = jnp.where(near + far == length - 1, 1.0, 0.0).astype(BF16)
    zero = jnp.zeros((), BF16)
    for pair in range(HEADS // 2):
        columns = slice(pair * 2 * depth, (pair + 1) * 2 * depth)
        grad_pair = None
        for side in range(2):
            mine = (lane < depth) if side == 0 else (lane >= depth)
            mixing = mixing_ref[2 * pair + side]
            grad_mixing = against(jnp.where(mine, context_grad[:, columns], zero), values_ref[:, columns])
            inner = jnp.sum(mixing * grad_mixing, axis=-1, keepdims=True)
            low = rounded(mixing * (grad_mixing - inner) * (1.0 / math.sqrt(depth)))
            head = 2 * pair + side
            scores[:, head * length : (head + 1) * length] = low
            parts = (
                product(low, keys_ref[:, columns]),
                across(low, query_u_ref[:, columns]),
                across(rounded(mixing), context_grad[:, columns]),
            )
            grad_pair = parts if side == 0 else tuple(jnp.where(mine, p, q) for p, q in zip(parts, grad_pair))
        grad_u[:, columns] = grad_pair[0]
        keys_low_ref[:, columns] = rounded(grad_pair[1])
        values_low_ref[:, columns] = rounded(grad_pair[2])
        vectors_ref[6:7, columns] = total_of(grad_pair[2])
    flipped = product(flip, scores[...])
    for head in range(HEADS):
        padded = jnp.concatenate(
            [flipped[:, head * length : (head + 1) * length], jnp.zeros((length, length), F32)], axis=1
        )
        wide_scores[:, head * 2 * length : (head + 1) * 2 * length] = rounded(
            pltpu.roll(padded, 0, 1, stride=1, stride_axis=0)
        )
    wide_scores[...] = rounded(product(flip, wide_scores[...]))
    for pair in range(HEADS // 2):
        columns = slice(pair * 2 * depth, (pair + 1) * 2 * depth)
        kept = None
        for side in range(2):
            head = 2 * pair + side
            low = wide_scores[:, head * 2 * length : (head + 1) * 2 * length]
            parts = (product(low, places_ref[:, columns]), across(low, query_v_ref[:, columns]))
            mine = (lane < depth) if side == 0 else (lane >= depth)
            tall = jnp.concatenate([mine, mine], axis=0)
            kept = parts if side == 0 else (jnp.where(mine, parts[0], kept[0]), jnp.where(tall, parts[1], kept[1]))
        grad_v[:, columns] = kept[0]
        places_grad_ref[:, columns] = kept[1]
    vectors_ref[7:8, :] = total_of(grad_u[...])
    vectors_ref[8:9, :] = total_of(grad_v[...])
    grad_query = grad_u[...] + grad_v[...]
    query_low = rounded(grad_query)
    query_low_ref[...] = query_low
    vectors_ref[5:6, :] = total_of(grad_query)
    grad_normed = (
        against(query_low, query_w_ref[...])
        + against(keys_low_ref[...], key_w_ref[...])
        + against(values_low_ref[...], value_w_ref[...])
    )
    pulled, gain_grad, shift_grad = norm_back(first_ref[...], row_of(table_ref, 3), grad_normed)
    vectors_ref[3:4, :] = gain_grad
    vectors_ref[4:5, :] = shift_grad
    first_grad_ref[...] = second_grad_ref[...] + pulled


def front_back_kernel(first_grad_ref, hidden_ref, shrink_ref, half_ref, hidden_low_ref, lift_ref, offset_ref):
    half = 0.5 * first_grad_ref[...]
    half_low = rounded(half)
    half_ref[...] = half_low
    offset_ref[...] = total_of(half)
    grad_hidden = against(half_low, shrink_ref[...]) * swish_slope(hidden_ref[...])
    lift_ref[...] = total_of(grad_hidden)
    hidden_low_ref[...] = rounded(grad_hidden)


def input_back_kernel(rows_ref, first_grad_ref, hidden_low_ref, expand_ref, table_ref, grad_ref, vectors_ref):
    pulled, gain_grad, shift_grad = norm_back(
        widened(rows_ref[...]), row_of(table_ref, 0), against(hidden_low_ref[...], expand_ref[...])
    )
    vectors_ref[0:1, :] = gain_grad
    vectors_ref[1:2, :] = shift_grad
    grad_ref[...] = first_grad_ref[...] + pulled


def collect_kernel(devices, width, plans, me_ref, *refs):
    count = len(plans[0]) + len(plans[1])
    factors, halves, held = refs[: 2 * count], refs[2 * count : 2 * count + 4], refs[2 * count + 4 :]
    orders = stage_orders(devices)
    me = me_ref[0]
    for item in range(count):
        left, right = factors[2 * item][...], factors[2 * item + 1]
        for start in range(0, right.shape[1], width):
            columns = slice(start, start + width)
            if right.dtype == F32:
                high = rounded(right[:, columns])
                low = rounded(right[:, columns] - widened(high))
                held[item][:, columns] = rounded(across(left, high) + across(left, low))
            else:
                held[item][:, columns] = rounded(across(left, right[:, columns]))
    for colour in range(2):
        base = colour * len(plans[0])
        for core in range(2):
            target = halves[2 * colour + core]
            for position in range(devices // 2):
                owner = me ^ (relative(position, orders[colour]) ^ core)
                for item, (rows, blocks, offset) in enumerate(plans[colour]):
                    start = pl.multiple_of(owner * rows, rows)
                    for k in range(blocks):
                        target[position, offset + k * rows : offset + (k + 1) * rows, :] = held[base + item][
                            pl.ds(start, rows), k * width : (k + 1) * width
                        ]


def collect(me, pairs_a, pairs_b, width, devices):
    shapes = [[(a.shape[1] // devices, b.shape[1]) for a, b in pairs] for pairs in (pairs_a, pairs_b)]
    plans = tuple(plan_of(s, width) for s in shapes)
    heights = [sum(rows * blocks for rows, blocks, _ in plan) for plan in plans]
    pairs = list(pairs_a) + list(pairs_b)
    return whole(
        partial(collect_kernel, devices, width, plans),
        [((devices // 2, heights[colour], width), BF16) for colour in (0, 0, 1, 1)],
        [me] + [factor for pair in pairs for factor in pair],
        [pltpu.VMEM((a.shape[1], b.shape[1]), BF16) for a, b in pairs],
        "collect",
        True,
    )


def shard_of(rows, shapes, width):
    shards, offset = [], 0
    for height, columns in shapes:
        blocks = columns // width
        pieces = [rows[offset + k * height : offset + (k + 1) * height] for k in range(blocks)]
        shards.append(pieces[0] if blocks == 1 else jnp.concatenate(pieces, axis=1))
        offset += height * blocks
    return shards


def own_of(rows, me, own):
    return lax.dynamic_slice(rows, (0, me * own), (rows.shape[0], own))


def local_fast(inputs, *rest):
    params, cotangent = rest[:-1], rest[-1]
    (front_gain, front_shift, front_expand, front_lift, front_shrink, front_offset) = params[0:6]
    (
        attend_gain,
        attend_shift,
        query_w,
        query_b,
        key_w,
        value_w,
        value_b,
        place_w,
        content_b,
        place_b,
        output_w,
        output_b,
    ) = params[6:18]
    (
        module_gain,
        module_shift,
        gating_w,
        gating_b,
        depth_w,
        batch_gain,
        batch_shift,
        mixer_w,
        mixer_b,
    ) = params[18:27]
    (rear_gain, rear_shift, rear_expand, rear_lift, rear_shrink, rear_offset) = params[27:33]
    final_gain, final_shift = params[33:35]

    devices = lax.axis_size(AXIS)
    sequences, length, width = inputs.shape
    count = devices * sequences * length
    own = front_gain.shape[0]
    taps = depth_w.shape[1]
    index = lax.axis_index(AXIS)
    me = index.astype(jnp.int32).reshape(1)

    singles = jnp.stack(
        [
            front_gain, front_shift, front_offset,
            attend_gain, attend_shift, query_b, value_b, content_b, place_b, output_b,
            module_gain, module_shift, batch_gain, batch_shift, mixer_b,
            rear_gain, rear_shift, rear_offset, final_gain, final_shift,
        ],
        axis=0,
    )
    singles = jnp.pad(singles, ((0, 0), (0, 128 - own)))
    wide = [jnp.pad(v, (0, 128 - v.shape[0]))[None] for v in (front_lift, rear_lift, gating_b)]
    depth_rows = jnp.pad(depth_w.T, ((0, 2 * TILE_ROWS - taps), (0, 128 - own)))
    rows64 = jnp.concatenate(
        [singles] + wide + [jnp.zeros((2 * TILE_ROWS - 23, 128), singles.dtype), depth_rows], axis=0
    )
    vector_block = jnp.concatenate(
        [rows64[k * TILE_ROWS : (k + 1) * TILE_ROWS] for k in range(4)], axis=1
    )

    shapes = {
        "front_a": [front_expand.shape],
        "front_b": [front_shrink.shape],
        "middle_a": [gating_w.shape, query_w.shape, key_w.shape],
        "middle_b": [mixer_w.shape, value_w.shape, place_w.shape, output_w.shape],
        "rear_a": [rear_expand.shape],
        "rear_b": [rear_shrink.shape],
    }

    def stacked(*weights):
        return jnp.concatenate([piece for w in weights for piece in block_of(w, width)], axis=0)

    front_gather = Gather(
        jnp.concatenate([stacked(front_expand), vector_block], axis=0), stacked(front_shrink), devices
    )
    middle_gather = Gather(
        stacked(gating_w, query_w, key_w), stacked(mixer_w, value_w, place_w, output_w), devices
    )
    rear_gather = Gather(stacked(rear_expand), stacked(rear_shrink), devices)
    while front_gather.stage < front_gather.heads:
        front_gather.advance()
    tie_stages(front_gather, middle_gather)
    for _ in range(2):
        front_gather.advance()
        middle_gather.advance()
        tie_stages(front_gather, middle_gather)
    tie_stages(front_gather, middle_gather, rear_gather)
    front_gather.advance()
    middle_gather.advance()
    rear_gather.advance()
    tie_stages(front_gather, middle_gather, rear_gather)
    middle_gather.advance()
    rear_gather.advance()

    rows = sequences * length
    front_expand, front_shrink, table, lifts, gates_bias = spread(
        me, front_gather.state, shapes["front_a"], shapes["front_b"], width, devices, stacked(params[2]).shape[0]
    )
    rows_in = inputs.reshape(rows, width)
    hidden_width = front_expand.shape[1]
    first, normed0, hidden0, active0 = whole(
        front_kernel,
        [((rows, width), F32), ((rows, width), BF16), ((rows, hidden_width), F32), ((rows, hidden_width), BF16)],
        [rows_in, table, lifts, front_expand, front_shrink],
        name="front",
    )
    (first, normed0, hidden0, active0), middle_gather.state, rear_gather.state = tie(
        (first, normed0, hidden0, active0), middle_gather.state, rear_gather.state
    )
    middle_gather.advance()
    rear_gather.advance()

    gating_w, query_w, key_w, mixer_w, value_w, place_w, output_w = spread(
        me, middle_gather.state, shapes["middle_a"], shapes["middle_b"], width, devices
    )
    (gating_w, query_w, key_w, mixer_w, value_w, place_w, output_w), rear_gather.state = tie(
        (gating_w, query_w, key_w, mixer_w, value_w, place_w, output_w), rear_gather.state
    )
    rear_gather.advance()
    angles = place_table(length, width)
    places = rounded(product(angles, place_w))
    pad = pltpu.VMEM((rows + 2 * TILE_ROWS, width), F32)
    (
        second, normed1, keys, values, query_u, query_v, mixing, context, normed2, gates, depth_out, stats,
    ) = whole(
        partial(attention_kernel, taps),
        [((rows, width), F32)] + [((rows, width), BF16)] * 5 + [((HEADS, length, length), F32)]
        + [((rows, width), BF16)] * 2 + [((rows, 2 * width), F32), ((rows, width), F32), ((2, width), F32)],
        [first, places, table, gates_bias, query_w, key_w, value_w, output_w, gating_w],
        [pad],
        "attention",
    )
    stats, rear_gather.state = tie(stats, rear_gather.state)
    rear_gather.advance()
    sums = Sum(stats, devices)
    sums.advance()
    rear_expand, rear_shrink = spread(me, rear_gather.state, shapes["rear_a"], shapes["rear_b"], width, devices)
    sums.state, (rear_expand, rear_shrink) = tie(sums.state, (rear_expand, rear_shrink))
    sums = sums.finish()
    (
        outputs, third_grad, normal_grad, normal, stats2, late_vectors, rear_lift_grad,
        normed3, hidden_low3, active3, half_low3, activated, third_low,
    ) = whole(
        partial(rear_kernel, count),
        [((rows, width), F32)] * 4 + [((2, width), F32), ((10, width), F32), ((1, hidden_width), F32)]
        + [((rows, width), BF16), ((rows, hidden_width), BF16), ((rows, hidden_width), BF16)]
        + [((rows, width), BF16)] * 3,
        [second, depth_out, sums, table, lifts, mixer_w, rear_expand, rear_shrink, cotangent.reshape(rows, width)],
        name="rear",
    )
    sums2 = Sum(stats2, devices)
    sums2.advance()
    halves = collect(me, [(normed3, hidden_low3)], [(active3, half_low3), (activated, third_low)], width, devices)
    sums2.state, halves = tie(sums2.state, halves)
    sums2.advance()
    rear_reduce = Reduce(halves, devices)
    tie_stages(sums2, rear_reduce)
    rear_reduce.advance()
    sums2.finish()
    tie_stages(sums2, rear_reduce)
    rear_reduce.advance()
    (sums2,) = sums2.state
    second_grad, second_low, gates_low, module_vectors, gates_bias_grad, taps_grad = whole(
        partial(module_back_kernel, count, taps),
        [((rows, width), F32), ((rows, width), BF16), ((rows, 2 * width), BF16), ((2, width), F32),
         ((1, 2 * width), F32), ((taps, width), F32)],
        [third_grad, normal_grad, normal, sums, sums2, table, gates, second, gating_w],
        [pad, pad],
        "module_back",
    )
    (second_grad, second_low), rear_reduce.state = tie((second_grad, second_low), rear_reduce.state)
    rear_reduce.advance()
    late_rows = jnp.concatenate(
        [
            module_vectors, late_vectors[2:],
            rear_lift_grad.reshape(4, width), gates_bias_grad.reshape(2, width), taps_grad,
        ],
        axis=0,
    )
    late = Sum(late_rows, devices)
    late.advance()
    first_grad, query_low, keys_low, values_low, places_grad, attend_vectors = whole(
        attention_back_kernel,
        [((rows, width), F32)] + [((rows, width), BF16)] * 3 + [((2 * length, width), F32), ((10, width), F32)],
        [second_grad, second_low, first, table, places, keys, values, query_u, query_v, mixing, output_w,
         query_w, key_w, value_w],
        [pltpu.VMEM((rows, HEADS * length), BF16), pltpu.VMEM((rows, width), BF16),
         pltpu.VMEM((rows, HEADS * 2 * length), BF16), pltpu.VMEM((rows, width), F32), pltpu.VMEM((rows, width), F32)],
        "attention_back",
    )
    back = (first_grad, query_low, keys_low, values_low, places_grad)
    back, rear_reduce.state, late.state = tie(back, rear_reduce.state, late.state)
    first_grad, query_low, keys_low, values_low, places_grad = back
    rear_reduce.advance()
    late.advance()
    halves = collect(
        me,
        [(normed2, gates_low), (normed1, query_low), (normed1, keys_low)],
        [(normed1, values_low), (angles, places_grad), (context, second_low)],
        width,
        devices,
    )
    halves, first_grad = tie(halves, first_grad)
    middle_reduce = Reduce(halves, devices)
    half_low0, hidden_low0, front_lift_grad, front_offset_grad = whole(
        front_back_kernel,
        [((rows, width), BF16), ((rows, hidden_width), BF16), ((1, hidden_width), F32), ((1, width), F32)],
        [first_grad, hidden0, front_shrink],
        name="front_back",
    )
    (half_low0, hidden_low0), middle_reduce.state, late.state, rear_reduce.state = tie(
        (half_low0, hidden_low0), middle_reduce.state, late.state, rear_reduce.state
    )
    middle_reduce.advance()
    halves = collect(me, [(normed0, hidden_low0)], [(active0, half_low0)], width, devices)
    halves, hidden_low0 = tie(halves, hidden_low0)
    front_reduce = Reduce(halves, devices)
    late.advance(2)
    grad_input, front_vectors = whole(
        input_back_kernel,
        [((rows, width), F32), ((2, width), F32)],
        [rows_in, first_grad, hidden_low0, front_expand, table],
        name="input_back",
    )
    early_rows = jnp.concatenate(
        [front_vectors, front_offset_grad, attend_vectors[3:], front_lift_grad.reshape(4, width)], axis=0
    )
    early = Sum(early_rows, devices)
    tie_stages(front_reduce, middle_reduce, late, early)
    early.advance()
    front_reduce.advance()
    middle_reduce.advance()
    late.advance()
    tie_stages(front_reduce, middle_reduce, early)
    early.advance()
    front_reduce.advance()
    middle_reduce.advance()
    tie_stages(front_reduce, middle_reduce, early)
    early.advance(2)
    front_reduce.advance()
    middle_reduce.advance()
    tie_stages(front_reduce, early)
    front_reduce.advance()
    early_sum, late_sum = early.finish(), late.finish()
    front_done, middle_done, rear_done = front_reduce.result(), middle_reduce.result(), rear_reduce.result()

    late_own = own_of(late_sum, index, own)
    early_own = own_of(early_sum, index, own)
    front_lift_own = lax.dynamic_slice(early_sum[10:14].reshape(-1), (index * 4 * own,), (4 * own,))
    rear_lift_own = lax.dynamic_slice(late_sum[10:14].reshape(-1), (index * 4 * own,), (4 * own,))
    gating_b_own = lax.dynamic_slice(late_sum[14:16].reshape(-1), (index * 2 * own,), (2 * own,))
    taps_own = late_own[16 : 16 + taps].T
    g_front_expand, g_front_shrink = shard_of(front_done, shapes["front_a"] + shapes["front_b"], width)
    g_gating, g_query, g_key, g_value, g_place, g_output = shard_of(
        middle_done, shapes["middle_a"] + shapes["middle_b"][1:], width
    )
    g_rear_expand, g_rear_shrink, g_mixer = shard_of(
        rear_done, shapes["rear_a"] + shapes["rear_b"] + shapes["middle_b"][:1], width
    )
    e, l = early_own, late_own
    return (
        outputs.reshape(sequences, length, width),
        grad_input.reshape(sequences, length, width),
        e[0], e[1], g_front_expand, front_lift_own, g_front_shrink, e[2],
        e[3], e[4], g_query, e[5], g_key, g_value, e[6], g_place, e[7], e[8], g_output, e[9],
        l[0], l[1], g_gating, gating_b_own, taps_own, l[2], l[3], g_mixer, l[4],
        l[5], l[6], g_rear_expand, rear_lift_own, g_rear_shrink, l[7],
        l[8], l[9],
    )


def local(inputs, *rest):
    devices = lax.axis_size(AXIS)
    own = rest[0].shape[0]
    width = inputs.shape[2]
    taps = rest[22].shape[1]
    packs = own % TILE_ROWS == 0 and 4 * own <= 128 and width == 4 * 128 and taps <= 2 * TILE_ROWS
    if devices >= 8 and devices & (devices - 1) == 0 and packs and inputs.shape[0] == 1:
        return local_fast(inputs, *rest)
    return local_plain(inputs, *rest)


def solution(mesh):
    placed = (
        P("fsdp", None, None),
        P("fsdp"),
        P("fsdp"),
        P("fsdp", None),
        P("fsdp"),
        P("fsdp", None),
        P("fsdp"),
        P("fsdp"),
        P("fsdp"),
        P("fsdp", None),
        P("fsdp"),
        P("fsdp", None),
        P("fsdp", None),
        P("fsdp"),
        P("fsdp", None),
        P("fsdp"),
        P("fsdp"),
        P("fsdp", None),
        P("fsdp"),
        P("fsdp"),
        P("fsdp"),
        P("fsdp", None),
        P("fsdp"),
        P("fsdp", None),
        P("fsdp"),
        P("fsdp"),
        P("fsdp", None),
        P("fsdp"),
        P("fsdp"),
        P("fsdp"),
        P("fsdp", None),
        P("fsdp"),
        P("fsdp", None),
        P("fsdp"),
        P("fsdp"),
        P("fsdp"),
        P("fsdp", None, None),
    )
    return jax.shard_map(
        local,
        mesh=mesh,
        in_specs=placed,
        out_specs=(
            P("fsdp", None, None),
            P("fsdp", None, None),
            P("fsdp"),
            P("fsdp"),
            P("fsdp", None),
            P("fsdp"),
            P("fsdp", None),
            P("fsdp"),
            P("fsdp"),
            P("fsdp"),
            P("fsdp", None),
            P("fsdp"),
            P("fsdp", None),
            P("fsdp", None),
            P("fsdp"),
            P("fsdp", None),
            P("fsdp"),
            P("fsdp"),
            P("fsdp", None),
            P("fsdp"),
            P("fsdp"),
            P("fsdp"),
            P("fsdp", None),
            P("fsdp"),
            P("fsdp", None),
            P("fsdp"),
            P("fsdp"),
            P("fsdp", None),
            P("fsdp"),
            P("fsdp"),
            P("fsdp"),
            P("fsdp", None),
            P("fsdp"),
            P("fsdp", None),
            P("fsdp"),
            P("fsdp"),
            P("fsdp"),
        ),
        check_vma=False,
    )
```
